32 devices in a mesh: cell: 8 (over z, y), grp: 4 (over x, core).
Axes of the slice: x: 2, y: 2, z: 4, core: 2. Of those that a mesh axis runs over, the one named last changes fastest.
Arguments:
- initial_guess: float32 [9, 6144], P(None, 'cell'), may hold values from -3 to 3
- right_side: float32 [9, 6144], P(None, 'cell')
- camera_blocks: float32 [9, 9, 6144], P(None, None, 'cell'), as said below
- point_inverse: float32 [3, 3, 16384], P(None, None, ('cell', 'grp')), as said below
- jacobian_tiles: bfloat16 [192, 576, 384], P(('cell', 'grp'))
- tile_pattern: int32 [192, 2], P(('cell', 'grp')), may hold values from 0 to 35, as said below
- cell_load: int32 [8], P('cell'), may hold values from 2 to 6, as said below
Outputs:
- solution: float32 [9, 6144], P(None, 'cell')
- residual: float32 [9, 6144], P(None, 'cell')
The draws below stay inside these ranges and needn't reach their ends.
Inputs may be any that keep to these rules, and one draw needn't show every extreme that they name: `tile_pattern`: column 0 is below 36, column 1 below 4. `cell_load`: A quarter of the cells, rounded down, chosen from the seed, have 6 live slots on each of their devices; every other cell has 2. Slots at or past the load are unused. `camera_blocks`: each camera block is symmetric with a dominant diagonal. `point_inverse`: each point's block is symmetric with a dominant diagonal.
All inputs are finite; a program needn't handle non-finite values.
Results may differ from the reference program's by a relative error of at most 0.0095.
Values may be sent and summed in bfloat16 or wider, within the bound.
A program may use at most 64 MiB of HBM per device.

```python
import math
from functools import partial
import jax
import jax.numpy as jnp
from jax import lax

CAM_PARAMS = 9
PT_PARAMS = 3
CAM_TILE = 64
PT_TILE = 128
CAM_TILES = 12
PT_TILES = 4
SLOTS = 6
ITERS = 2
CELLS = 8
GRPS = 4
CAMERAS = 6144
POINTS = 16384
TILES = 192


def draw_right_side(key, part):
    position = jnp.arange(CAMERAS, dtype=jnp.float32) / CAMERAS
    rising = jnp.exp(math.log(3.0) * position)[None, :]
    return jax.random.truncated_normal(key, -4.0, 4.0, (CAM_PARAMS, CAMERAS), jnp.float32) * rising


def symmetric_blocks(key, size, columns, offset, low, high):
    raw = jax.random.uniform(key, (size, size, columns), jnp.float32, -offset, offset)
    mirrored = 0.5 * (raw + raw.transpose(1, 0, 2))
    diagonal = jax.random.uniform(jax.random.fold_in(key, 7), (size, columns), jnp.float32, low, high)
    identity = (jnp.arange(size)[:, None] == jnp.arange(size)[None, :]).astype(jnp.float32)
    return mirrored * (1.0 - identity)[:, :, None] + identity[:, :, None] * diagonal[:, None, :]


def draw_camera_blocks(key, part):
    return symmetric_blocks(key, CAM_PARAMS, CAMERAS, 0.06, 1.5, 3.0)


def draw_point_inverse(key, part):
    return symmetric_blocks(key, PT_PARAMS, POINTS, 0.15, 0.5, 1.0)


def draw_jacobian_tiles(key, part):
    rows = CAM_PARAMS * CAM_TILE
    columns = PT_PARAMS * PT_TILE
    half = 0.3 * math.sqrt(3.0) / math.sqrt(rows + columns)
    base = jax.random.uniform(key, (TILES, rows, columns), jnp.float32, -half, half)
    return base.astype(jnp.bfloat16)


def draw_tile_pattern(key, part):
    window = jax.random.randint(key, (TILES, 1), 0, 3 * CAM_TILES, dtype=jnp.int32)
    points = jax.random.randint(jax.random.fold_in(key, 5), (TILES, 1), 0, PT_TILES, dtype=jnp.int32)
    return jnp.concatenate([window, points], axis=1)


def draw_cell_load(key, part):
    ranking = jax.random.permutation(key, CELLS)
    return jnp.where(ranking < CELLS // 4, SLOTS, SLOTS // 3).astype(jnp.int32)


def block_scale(key, shape, pieces, smallest, top_value):
    gain, own = 1.0, jax.random.fold_in(key, 6)
    for axis_at, parts in pieces:
        heights = jnp.exp(jax.random.uniform(jax.random.fold_in(own, axis_at), (parts,), jnp.float32, smallest / len(pieces), top_value / len(pieces)))
        gain = gain * jnp.repeat(heights, shape[axis_at] // parts).reshape([-1 if axis == axis_at else 1 for axis in range(len(shape))])
    return gain


def centred(key, shape, width, limit, split=(), kind=jnp.bfloat16):
    drawn = width * jax.random.normal(key, shape, jnp.float32)
    if split:
        drawn = drawn * block_scale(key, shape, split, -0.22, 0.18)
    return jnp.clip(drawn, -limit, limit).astype(kind)


def setup_inputs(seed: int = 0) -> dict:
    seeds = jax.random.split(jax.random.key(seed), 8)
    initial_guess = centred(seeds[0], (CAM_PARAMS, CAMERAS), 0.5, 3.0, ((1, 8),), jnp.float32)
    right_side = draw_right_side(jax.random.fold_in(seeds[7], 71), 0)
    camera_blocks = draw_camera_blocks(jax.random.fold_in(seeds[7], 71), 0)
    point_inverse = draw_point_inverse(jax.random.fold_in(seeds[7], 71), 0)
    jacobian_tiles = draw_jacobian_tiles(jax.random.fold_in(seeds[7], 71), 0)
    tile_pattern = draw_tile_pattern(jax.random.fold_in(seeds[7], 71), 0)
    cell_load = draw_cell_load(jax.random.fold_in(seeds[7], 71), 0)
    return dict(initial_guess=initial_guess, right_side=right_side, camera_blocks=camera_blocks, point_inverse=point_inverse, jacobian_tiles=jacobian_tiles, tile_pattern=tile_pattern, cell_load=cell_load)


HIGHEST = lax.Precision.HIGHEST


def tile_rows(camera_field, tile_width):
    components = camera_field.shape[0]
    return camera_field.reshape(components, -1, tile_width).transpose(1, 0, 2).reshape(-1, components * tile_width)


def schur_apply(direction, camera_blocks, point_inverse, jacobian_tiles, tile_pattern, cell_load):
    lowered = direction.astype(jnp.bfloat16)
    camera_rows = tile_rows(lowered, CAM_TILE)
    devices = CELLS * GRPS
    tiles_dev = jacobian_tiles.reshape(devices, SLOTS, CAM_PARAMS * CAM_TILE, PT_PARAMS * PT_TILE)
    pattern_dev = tile_pattern.reshape(devices, SLOTS, 2)
    inverse_dev = point_inverse.reshape(PT_PARAMS, PT_PARAMS, devices, PT_TILES, PT_TILE).transpose(2, 0, 1, 3, 4)

    def one_device(device_items):
        device, device_tiles, pattern, inverse = device_items
        cell_index = device // GRPS
        window = pattern[:, 0]
        cam_tile = ((cell_index - 1 + window // CAM_TILES) % CELLS) * CAM_TILES + window % CAM_TILES
        cam_tile = cam_tile.astype(jnp.int32)
        live_mask = (jnp.arange(SLOTS, dtype=jnp.int32) < cell_load[cell_index]).astype(jnp.float32)
        tiles_wide = device_tiles.astype(jnp.float32)
        chosen = camera_rows[cam_tile].astype(jnp.float32)
        forward = jnp.einsum("tk,tkj->tj", chosen, tiles_wide, precision=HIGHEST) * live_mask[:, None]
        point_sums = jax.ops.segment_sum(forward, pattern[:, 1], PT_TILES)
        solved = jnp.einsum("jipq,piq->pjq", inverse, point_sums.reshape(PT_TILES, PT_PARAMS, PT_TILE), precision=HIGHEST)
        solved = solved.reshape(PT_TILES, PT_PARAMS * PT_TILE).astype(jnp.bfloat16)
        gathered = solved[pattern[:, 1]].astype(jnp.float32)
        backward = jnp.einsum("tj,tkj->tk", gathered, tiles_wide, precision=HIGHEST) * live_mask[:, None]
        return backward, cam_tile

    backward, cam_tile = lax.map(one_device, (jnp.arange(devices, dtype=jnp.int32), tiles_dev, pattern_dev, inverse_dev))
    back_rows = jax.ops.segment_sum(backward.reshape(-1, CAM_PARAMS * CAM_TILE), cam_tile.reshape(-1), CELLS * CAM_TILES)
    back_field = back_rows.reshape(CELLS * CAM_TILES, CAM_PARAMS, CAM_TILE).transpose(1, 0, 2).reshape(CAM_PARAMS, -1)
    return jnp.einsum("klc,lc->kc", camera_blocks, direction, precision=HIGHEST) - back_field


def reference(initial_guess, right_side, camera_blocks, point_inverse, jacobian_tiles, tile_pattern, cell_load):
    operate = partial(schur_apply, camera_blocks=camera_blocks, point_inverse=point_inverse, jacobian_tiles=jacobian_tiles, tile_pattern=tile_pattern, cell_load=cell_load)
    diagonal_part = jnp.diagonal(camera_blocks, axis1=0, axis2=1).T
    solution = initial_guess
    residual = right_side - operate(solution)
    precond = residual / diagonal_part
    direction = precond
    rz_now = jnp.sum(residual * precond)
    for iteration in range(ITERS):
        image = operate(direction)
        step_size = rz_now / jnp.sum(direction * image)
        solution = solution + step_size * direction
        residual = residual - step_size * image
        precond = residual / diagonal_part
        rz_next = jnp.sum(residual * precond)
        direction = precond + (rz_next / rz_now) * direction
        rz_now = rz_next
    return solution, residual
```

```python
import functools

import jax
import jax.numpy as jnp
from jax import lax
from jax.experimental import pallas as pl
from jax.experimental.pallas import tpu as pltpu
from jax.sharding import PartitionSpec as P

CAM_TILE = 64
REACH = 2
SPAN = 2 * REACH + 1
ORDER = sorted(range(-REACH, REACH + 1), key=abs)
LANES = 128
ROWS = 8
PACK = 32
NONE = -(1 << 20)
MESH = pl.DeviceIdType.MESH
F32 = jnp.float32
BF16 = jnp.bfloat16
I32 = jnp.int32


def round_up(value, step):
    return (value + step - 1) // step * step


def kernel(
    cells,
    grps,
    guess_hbm,
    right_hbm,
    blocks_hbm,
    inverse_hbm,
    jac_hbm,
    pattern_hbm,
    load_hbm,
    solution_ref,
    residual_ref,
    pattern,
    load,
    guess,
    right,
    blocks,
    inverse,
    jac,
    fields,
    keys,
    slot_send,
    slot_recv,
    scalar_send,
    scalar_recv,
    choose_slots,
    choose_field,
    choose_window,
    local_sem,
    jac_sem,
    field_send_sem,
    field_recv_sem,
    key_send_sem,
    key_recv_sem,
    slot_send_sem,
    slot_recv_sem,
    scalar_sem,
):
    params, cameras = guess.shape
    slots, rows_wide, points_wide = jac.shape
    tiles = cameras // CAM_TILE
    pairs = cameras // LANES
    coords = inverse.shape[0]
    point_tiles = inverse.shape[2] // LANES
    full = rows_wide // LANES
    slot_rows_sent = round_up(full * slots + slots // 2, 4)
    field_rows = full * tiles + tiles // 2
    field_rows_sent = round_up(field_rows, ROWS)
    field_pack = fields.shape[2]
    near_count = SPAN * grps
    close_count = 3 * grps
    devices = cells * grps
    cell = lax.axis_index("cell")
    grp = lax.axis_index("grp")

    def near(delta, turn):
        return (lax.rem(cell + delta + cells, cells), lax.rem(grp + turn + grps, grps))

    def slot_index(delta, turn):
        return ORDER.index(delta) * grps + turn % grps

    peers = sorted(
        [(d, t) for d in ORDER for t in range(grps) if (d, t) != (0, 0)],
        key=lambda peer: ((abs(peer[0]) + REACH) % (REACH + 1), -peer[1]),
    )
    first_wave = [(d, t) for d, t in peers if d == 0 or t == 0]
    second_wave = [(d, t) for d, t in peers if d != 0 and t != 0]
    key_index = {(0, 0): 0}
    for delta, turn in first_wave + second_wave:
        key_index[(delta, turn)] = len(key_index)

    turned = [lax.rem(grp + turn, grps) for turn in range(grps)]

    def everyone(act):
        for turn in range(1, grps):
            act(turn - 1, (cell, turned[turn]))

        def one_cell(delta, carry):
            other = lax.rem(cell + delta, cells)
            for turn in range(grps):
                act(delta * grps + (turn - 1), (other, turned[turn]))
            return carry

        lax.fori_loop(1, cells, one_cell, 0)

    barrier = pltpu.get_barrier_semaphore()

    def greet(index, device):
        pl.semaphore_signal(barrier, inc=1, device_id=device, device_id_type=MESH)

    if cells // 2 <= 2 * REACH:
        greeted = len(first_wave)
        for delta, turn in first_wave:
            greet(0, near(delta, turn))
    else:
        greeted = devices - 1
        everyone(greet)

    local = [
        pltpu.make_async_copy(src, dst, local_sem.at[i])
        for i, (src, dst) in enumerate(
            (
                (guess_hbm, guess),
                (pattern_hbm, pattern),
                (load_hbm, load),
                (blocks_hbm, blocks),
                (right_hbm, right),
                (inverse_hbm, inverse),
            )
        )
    ]
    jac_copies = [
        pltpu.make_async_copy(jac_hbm.at[s], jac.at[s], jac_sem.at[s]) for s in range(slots)
    ]
    for copy in local:
        copy.start()
    for copy in jac_copies:
        copy.start()

    def iota(shape, axis):
        return lax.broadcasted_iota(I32, shape, axis)

    def steps(value, width, count):
        return sum((value >= width * j).astype(I32) for j in range(1, count + 1))

    lane8 = iota((ROWS, LANES), 1)
    row8 = iota((ROWS, LANES), 0)
    low8 = lane8 < CAM_TILE
    low1 = iota((1, LANES), 1) < CAM_TILE
    even8 = lax.bitwise_and(row8, 1) == 0

    fields[:, :, field_rows_sent:, :] = jnp.zeros(
        (fields.shape[0], 3, field_pack - field_rows_sent, LANES), BF16
    )
    slot_recv[:, :, slot_rows_sent:, :] = jnp.zeros(
        (3, near_count, PACK - slot_rows_sent, LANES), BF16
    )

    pick_row = iota((field_pack, LANES), 0)
    pick_chunk = steps(pick_row, tiles, full)
    pick_tile = pick_row - pick_chunk * tiles
    pick_tail = pick_chunk == full
    source_low = 16 * pick_tile + 2 * pick_chunk
    other_tile = jnp.where(pick_tail, pick_tile + tiles // 2, pick_tile)
    flipped = other_tile + 1 - 2 * lax.bitwise_and(other_tile, 1)
    source_high = 16 * flipped + jnp.where(pick_tail, 2 * full, 2 * pick_chunk + 1)
    unused = pick_row >= field_rows
    source_low = jnp.where(unused, -1, source_low)
    source_high = jnp.where(unused, -1, source_high)
    picked_width = 16 * tiles
    lane_pick = iota((field_pack, LANES), 1)

    def one_hot(source):
        parts = [
            (source == lane_pick + LANES * j).astype(F32)
            for j in range(round_up(picked_width, LANES) // LANES)
        ]
        return jnp.concatenate(parts, axis=1)[:, :picked_width].astype(BF16)

    spread = jnp.concatenate([one_hot(source_low), one_hot(source_high)], axis=0)

    def to_rows(field):
        tall = jnp.concatenate([field, jnp.zeros((16 - params, cameras), F32)], axis=0)
        parts = []
        for i in range(pairs):
            block = tall[:, i * LANES : (i + 1) * LANES]
            parts += [block.astype(BF16), pltpu.roll(block, CAM_TILE, 1).astype(BF16)]
        both = jnp.dot(spread, jnp.concatenate(parts, axis=0), preferred_element_type=F32)
        low = lane_pick < CAM_TILE
        picked = jnp.where(low, both[:field_pack], both[field_pack:])
        return picked[:field_rows_sent].astype(BF16)

    def put_field(f, field):
        fields[f, 2, :field_rows_sent] = to_rows(field)

    def field_copies(f):
        return [
            pltpu.make_async_remote_copy(
                src_ref=fields.at[f, 2, pl.ds(0, field_rows_sent)],
                dst_ref=fields.at[f, side, pl.ds(0, field_rows_sent)],
                send_sem=field_send_sem.at[f],
                recv_sem=field_recv_sem.at[f],
                device_id=near(delta, 0),
                device_id_type=MESH,
            )
            for side, delta in ((0, 1), (1, -1))
        ]

    def wait_bytes(ref, sem):
        pltpu.make_async_copy(ref, ref, sem).wait()

    def field_bytes(f, sem):
        wait_bytes(fields.at[f, pl.ds(0, 2), pl.ds(0, field_rows_sent)], sem.at[f])

    local[0].wait()
    put_field(0, guess[...])

    local[1].wait()
    local[2].wait()
    live = [s < load[0] for s in range(slots)]
    ids = [pattern[0, s] for s in range(slots)]
    point_ids = [pattern[1, s] for s in range(slots)]
    live_rows = jnp.zeros((ROWS, LANES), I32)
    id_rows = jnp.full((ROWS, LANES), NONE, I32)
    point_rows = jnp.full((ROWS, LANES), -1, I32)
    first_rows = jnp.zeros((ROWS, LANES), F32)
    for s in range(slots):
        here = row8 == s
        id_rows = jnp.where(here, jnp.where(live[s], 8 * ids[s], NONE), id_rows)
        point_rows = jnp.where(here, point_ids[s], point_rows)
        live_rows = jnp.where(here, jnp.where(live[s], 1, 0), live_rows)
        first = live[s]
        for u in range(s):
            same = jnp.logical_and(live[u], point_ids[u] == point_ids[s])
            first = jnp.logical_and(first, jnp.logical_not(same))
        first_rows = jnp.where(here, jnp.where(first, 1.0, 0.0), first_rows)
    live8 = live_rows > 0
    shared = [
        jnp.logical_and(point_rows == point_ids[s], jnp.where(live[s], 1, 0) > 0)
        for s in range(slots)
    ]

    key_lane = lax.bitwise_and(iota((2, LANES), 1), PACK - 1)
    key_chunk = steps(key_lane, slots, full)
    key_slot = key_lane - slots * key_chunk
    key_row = iota((2, LANES), 0)
    key_tail = jnp.logical_and(key_chunk == full, key_slot < slots // 2)
    own_key = jnp.full((2, LANES), NONE, I32)
    for s in range(slots):
        code = jnp.where(live[s], 8 * ids[s], NONE)
        head = jnp.logical_and(jnp.logical_and(key_chunk < full, key_slot == s), key_row == 0)
        tail_row, tail_slot = divmod(s, slots // 2)
        tail = jnp.logical_and(
            jnp.logical_and(key_tail, key_slot == tail_slot), key_row == tail_row
        )
        own_key = jnp.where(head, code + key_chunk, own_key)
        own_key = jnp.where(tail, code + full + tail_row, own_key)
    keys[0] = own_key

    row_keys = [id_rows + b for b in range(full + 2)]

    window_lane = iota((1, LANES), 1)
    window_parts = [[], []]
    window_width = 3 * field_pack
    for group in range(round_up(window_width, LANES) // LANES):
        position = window_lane + LANES * group
        place = steps(position, field_pack, 2)
        side = jnp.where(place == 0, 0, jnp.where(place == 1, 2, 1))
        row = position - place * field_pack
        chunk = steps(row, tiles, full)
        tile = side * tiles + row - chunk * tiles
        off = row >= field_rows
        tail = jnp.logical_and(chunk == full, jnp.logical_not(off))
        window_parts[0].append(jnp.where(off, -1, 8 * tile + chunk))
        window_parts[1].append(jnp.where(tail, 8 * (tile + tiles // 2) + full + 1, -1))
    window_low = window_parts[0]
    window_high = window_parts[1]

    def matches(low_keys, high_keys):
        parts = []
        for b in range(full + 2):
            found = low_keys if b <= full else high_keys
            parts.append(
                jnp.concatenate([(key == row_keys[b]).astype(F32) for key in found], axis=1)
            )
        return jnp.concatenate(parts, axis=0).astype(BF16)

    choose_window[...] = matches(window_low, window_high)[:, :window_width]

    def slot_fields(chosen, rows):
        found = jnp.dot(chosen, rows, preferred_element_type=F32)
        parts = [found[b * ROWS : (b + 1) * ROWS] for b in range(full + 2)]
        tail = parts[full] + pltpu.roll(parts[full + 1], CAM_TILE, 1)
        return jnp.concatenate(parts[:full] + [tail], axis=1)[:, :rows_wide]

    def window_slots(f):
        return slot_fields(choose_window[...], fields[f].reshape(window_width, LANES))

    def block_product(field):
        total = blocks[0] * field[0:1, :]
        for k in range(1, params):
            total = total + blocks[k] * field[k : k + 1, :]
        return total

    local[3].wait()
    row_wide = iota((params, cameras), 0)
    diagonal = blocks[0]
    for k in range(1, params):
        diagonal = jnp.where(row_wide == k, blocks[k], diagonal)
    scale = 1.0 / diagonal
    local[4].wait()
    residual0 = right[...] - block_product(guess[...])
    put_field(1, residual0 * scale)
    put_field(2, scale)
    local[5].wait()
    inverse_rows = []
    for j in range(coords):
        for i in range(coords):
            picked = jnp.zeros((ROWS, LANES), F32)
            for q in range(point_tiles):
                picked = jnp.where(
                    point_rows == q, inverse[j, i : i + 1, q * LANES : (q + 1) * LANES], picked
                )
            inverse_rows.append(picked)

    for copy in jac_copies:
        copy.wait()
    pl.semaphore_wait(barrier, greeted)

    for copy in field_copies(0):
        copy.start()

    def send_keys(wave, sem):
        for delta, turn in wave:
            pltpu.make_async_remote_copy(
                src_ref=keys.at[0],
                dst_ref=keys.at[key_index[(-delta, -turn % grps)]],
                send_sem=key_send_sem.at[sem],
                recv_sem=key_recv_sem.at[sem],
                device_id=near(delta, turn),
                device_id_type=MESH,
            ).start()

    first_keys = pl.ds(1, len(first_wave))
    second_keys = pl.ds(1 + len(first_wave), len(second_wave))
    send_keys(first_wave, 0)
    for f in (1, 2):
        for copy in field_copies(f):
            copy.start()

    def slot_rows(values):
        values = jnp.where(live_wide, values, 0.0)
        sums = jnp.zeros((ROWS, points_wide), F32)
        for s in range(slots):
            spread_row = jnp.where(shared_wide[s], values[s : s + 1, :], 0.0)
            sums = sums + jnp.dot(spread_row.astype(BF16), jac[s], preferred_element_type=F32)
        solved = []
        for j in range(coords):
            total = inverse_rows[j * coords] * sums[:, :LANES]
            for i in range(1, coords):
                total = total + inverse_rows[j * coords + i] * sums[:, i * LANES : (i + 1) * LANES]
            solved.append(total)
        solved = jnp.concatenate(solved, axis=1).astype(BF16).astype(F32)
        return sums, solved

    def slot_message(solved):
        parts = [jnp.zeros((ROWS, LANES), F32) for _ in range(PACK // ROWS)]
        tails = []
        for s in range(slots):
            row = jnp.broadcast_to(solved[s : s + 1, :], (ROWS, points_wide)).astype(BF16)
            product = lax.dot_general(
                row, jac[s], (((1,), (1,)), ((), ())), preferred_element_type=F32
            )
            product = jnp.where(live[s], product, 0.0)
            for b in range(full):
                at, inside = divmod(b * slots + s, ROWS)
                parts[at] = jnp.where(
                    row8 == inside, product[:, b * LANES : (b + 1) * LANES], parts[at]
                )
            tails.append(product[:, full * LANES :])
        for i in range(slots // 2):
            at, inside = divmod(full * slots + i, ROWS)
            both = jnp.concatenate([tails[i], tails[i + slots // 2]], axis=1)
            parts[at] = jnp.where(row8 == inside, both, parts[at])
        return jnp.concatenate(parts, axis=0).astype(BF16)

    def energy_of(sums, solved):
        energy = sums * solved
        lanes = energy[:, :LANES]
        for i in range(1, coords):
            lanes = lanes + energy[:, i * LANES : (i + 1) * LANES]
        return jnp.sum(lanes * first_rows, axis=0, keepdims=True)

    live_wide = jnp.concatenate([live8] * (full + 1), axis=1)[:, :rows_wide]
    shared_wide = [
        jnp.concatenate([shared[s]] * (full + 1), axis=1)[:, :rows_wide] for s in range(slots)
    ]

    def send_slots(turn_no, message, reach):
        slot_send[turn_no] = message
        slot_recv[turn_no, 0] = message
        for delta, turn in peers:
            if abs(delta) <= reach:
                pltpu.make_async_remote_copy(
                    src_ref=slot_send.at[turn_no, pl.ds(0, slot_rows_sent)],
                    dst_ref=slot_recv.at[
                        turn_no, slot_index(-delta, -turn), pl.ds(0, slot_rows_sent)
                    ],
                    send_sem=slot_send_sem.at[turn_no],
                    recv_sem=slot_recv_sem.at[turn_no],
                    device_id=near(delta, turn),
                    device_id_type=MESH,
                ).start()

    def wait_slots(turn_no, count, sem):
        wait_bytes(
            slot_recv.at[turn_no, pl.ds(1, count - 1), pl.ds(0, slot_rows_sent)], sem.at[turn_no]
        )

    def received(turn_no, count):
        return slot_recv[turn_no, :count].reshape(count * PACK, LANES)

    def own_back(turn_no, count):
        width = count * PACK
        found = jnp.dot(
            choose_field[:, :width], received(turn_no, count), preferred_element_type=F32
        )
        parts = []
        for i in range(pairs):
            first = found[32 * i : 32 * i + 16]
            second = found[32 * i + 16 : 32 * i + 32]
            first_turned = pltpu.roll(first, CAM_TILE, 1)
            second_turned = pltpu.roll(second, CAM_TILE, 1)
            top = jnp.where(
                low8,
                jnp.where(even8, first[:ROWS], first_turned[:ROWS]),
                jnp.where(even8, second_turned[:ROWS], second[:ROWS]),
            )
            last = jnp.where(
                low1,
                first[ROWS : ROWS + 1] + first_turned[ROWS + 1 : ROWS + 2],
                second_turned[ROWS : ROWS + 1] + second[ROWS + 1 : ROWS + 2],
            )
            parts.append(jnp.concatenate([top, last], axis=0))
        return jnp.concatenate(parts, axis=1)

    field_bytes(0, field_recv_sem)
    wait_bytes(keys.at[first_keys], key_recv_sem.at[0])
    send_keys(second_wave, 1)
    _, solved = slot_rows(window_slots(0))
    send_slots(0, slot_message(solved), REACH)

    wait_bytes(keys.at[second_keys], key_recv_sem.at[1])
    lows, highs = [], []
    place_lane = lax.shift_right_logical(window_lane, 5)
    per_group = LANES // PACK
    order = [(delta, turn) for delta in ORDER for turn in range(grps)]
    for group in range(near_count // per_group):
        low = jnp.full((1, LANES), NONE, I32)
        high = jnp.full((1, LANES), NONE, I32)
        for j in range(per_group):
            delta, turn = order[group * per_group + j]
            key = keys[key_index[(delta, turn)]] + 8 * tiles * delta
            low = jnp.where(place_lane == j, key[0:1], low)
            high = jnp.where(place_lane == j, key[1:2], high)
        lows.append(low)
        highs.append(high)
    choose_slots[...] = matches(lows, highs)
    half_row = lax.shift_right_logical(row8, 1)
    mixed = [jnp.where(row8 == 0, low, high) for low, high in zip(lows, highs)]
    for t in range(tiles):
        base = 8 * (tiles + t)
        top = jnp.concatenate([(low == base + half_row).astype(F32) for low in lows], axis=1)
        tail_key = jnp.where(row8 < 2, base + full + row8, -1)
        tail = jnp.concatenate([(mix == tail_key).astype(F32) for mix in mixed], axis=1)
        choose_field[16 * t : 16 * (t + 1)] = jnp.concatenate([top, tail], axis=0).astype(BF16)
    for f in (1, 2):
        field_bytes(f, field_recv_sem)
    start_slots = window_slots(1)
    scale_slots = window_slots(2)

    wait_slots(0, near_count, slot_recv_sem)
    back = slot_fields(choose_slots[...], received(0, near_count))
    direction_slots = start_slots + scale_slots * back
    _, solved = slot_rows(direction_slots)
    send_slots(1, slot_message(solved), REACH)
    field_bytes(1, field_send_sem)
    residual0 = residual0 + own_back(0, near_count)
    direction = residual0 * scale
    product1 = block_product(direction)
    put_field(3, (product1 - diagonal * direction) * scale)
    for copy in field_copies(3):
        copy.start()
    field_bytes(3, field_recv_sem)
    change_slots = window_slots(3)

    wait_slots(1, near_count, slot_recv_sem)
    back = slot_fields(choose_slots[...], received(1, near_count))
    sums, solved = slot_rows(scale_slots * back - change_slots)
    send_slots(2, slot_message(solved), 1)
    field_bytes(2, field_send_sem)
    energy = energy_of(sums, solved)
    image1 = product1 - own_back(1, near_count)
    trial = residual0 - image1
    shaped = trial * scale
    product2 = block_product(shaped)

    def lane_sum(field):
        total = field[:, :LANES]
        for i in range(1, pairs):
            total = total + field[:, i * LANES : (i + 1) * LANES]
        return jnp.sum(total, axis=0, keepdims=True) * (1.0 / grps)

    sums = jnp.zeros((ROWS, LANES), F32)
    for i, value in enumerate(
        (
            lane_sum(residual0 * direction),
            lane_sum(direction * image1),
            lane_sum(residual0 * shaped),
            lane_sum(trial * shaped),
            lane_sum(image1 * shaped),
            lane_sum(shaped * product2) - energy,
        )
    ):
        sums = jnp.where(row8 == i, value, sums)
    sums = jnp.sum(sums, axis=1, keepdims=True)
    own_sums = jnp.sum(jnp.where(row8 == lane8, sums, 0.0), axis=0, keepdims=True)
    scalar_send[...] = own_sums

    def send_scalars(index, device):
        pltpu.make_async_remote_copy(
            src_ref=scalar_send,
            dst_ref=scalar_recv.at[index],
            send_sem=scalar_sem.at[0],
            recv_sem=scalar_sem.at[1],
            device_id=device,
            device_id_type=MESH,
        ).start()

    everyone(send_scalars)

    wait_slots(2, close_count, slot_recv_sem)
    image2 = product2 - own_back(2, close_count)
    wait_bytes(scalar_recv, scalar_sem.at[1])
    totals = own_sums + jnp.sum(scalar_recv[...], axis=0)
    rz0, curve1, cross, trial_rz, mixed_sum, curve_w = [totals[:, i : i + 1] for i in range(6)]
    step1 = rz0 / curve1
    short = 1.0 - step1
    rz1 = short * short * rz0 + 2.0 * short * step1 * cross + step1 * step1 * trial_rz
    keep = short + rz1 / rz0
    curve2 = keep * keep * curve1 + 2.0 * keep * step1 * mixed_sum + step1 * step1 * curve_w
    step2 = rz1 / curve2
    near_part = step1 + step2 * keep
    far_part = step2 * step1
    solution_ref[...] = guess[...] + near_part * direction + far_part * shaped
    residual_ref[...] = residual0 - near_part * image1 - far_part * image2

    wait_bytes(scalar_recv, scalar_sem.at[0])
    for f in (0, 3):
        field_bytes(f, field_send_sem)
    wait_bytes(keys.at[first_keys], key_send_sem.at[0])
    wait_bytes(keys.at[second_keys], key_send_sem.at[1])
    for turn_no, count in enumerate((near_count, near_count, close_count)):
        wait_slots(turn_no, count, slot_send_sem)


def finish_kernel(first, second, solution_ref, residual_ref):
    solution_ref[...] = first[...]
    residual_ref[...] = second[...]


def finish(first, second):
    vmem = pl.BlockSpec(memory_space=pltpu.VMEM)
    shape = jax.ShapeDtypeStruct(first.shape, first.dtype)
    return pl.pallas_call(
        finish_kernel, out_shape=(shape, shape), in_specs=[vmem] * 2, out_specs=(vmem, vmem)
    )(*[pltpu.with_memory_space_constraint(x, pltpu.VMEM) for x in (first, second)])


def per_device(
    cells, grps, initial_guess, right_side, camera_blocks, point_inverse, jacobian_tiles, tile_pattern, cell_load
):
    params, cameras = initial_guess.shape
    slots, rows_wide, points_wide = jacobian_tiles.shape
    near = SPAN * grps
    tiles = cameras // CAM_TILE
    full = rows_wide // LANES
    field_pack = round_up(full * tiles + tiles // 2, 64)
    hbm = pl.BlockSpec(memory_space=pltpu.HBM)
    vmem = pl.BlockSpec(memory_space=pltpu.VMEM)
    dma = pltpu.SemaphoreType.DMA
    field = pltpu.VMEM((params, cameras), F32)
    first, second = pl.pallas_call(
        functools.partial(kernel, cells, grps),
        out_shape=(field, field),
        in_specs=[hbm] * 7,
        out_specs=(vmem, vmem),
        scratch_shapes=[
            pltpu.SMEM((2, slots), I32),
            pltpu.SMEM((1,), I32),
            pltpu.VMEM((params, cameras), F32),
            pltpu.VMEM((params, cameras), F32),
            pltpu.VMEM(camera_blocks.shape, F32),
            pltpu.VMEM(point_inverse.shape, F32),
            pltpu.VMEM(jacobian_tiles.shape, BF16),
            pltpu.VMEM((4, 3, field_pack, LANES), BF16),
            pltpu.VMEM((near, 2, LANES), I32),
            pltpu.VMEM((3, PACK, LANES), BF16),
            pltpu.VMEM((3, near, PACK, LANES), BF16),
            pltpu.VMEM((1, LANES), F32),
            pltpu.VMEM((cells * grps - 1, 1, LANES), F32),
            pltpu.VMEM((ROWS * (full + 2), near * PACK), BF16),
            pltpu.VMEM((16 * tiles, near * PACK), BF16),
            pltpu.VMEM((ROWS * (full + 2), 3 * field_pack), BF16),
            dma((6,)),
            dma((slots,)),
            dma((4,)),
            dma((4,)),
            dma((2,)),
            dma((2,)),
            dma((3,)),
            dma((3,)),
            dma((2,)),
        ],
        compiler_params=pltpu.CompilerParams(collective_id=0, has_side_effects=True),
    )(initial_guess, right_side, camera_blocks, point_inverse, jacobian_tiles, tile_pattern.T, cell_load)
    return finish(first, second)


def solution(mesh):
    placed = (
        P(None, "cell"),
        P(None, "cell"),
        P(None, None, "cell"),
        P(None, None, ("cell", "grp")),
        P(("cell", "grp"), None, None),
        P(("cell", "grp"), None),
        P("cell"),
    )
    return jax.shard_map(
        functools.partial(per_device, mesh.shape["cell"], mesh.shape["grp"]),
        mesh=mesh,
        in_specs=placed,
        out_specs=(P(None, "cell"), P(None, "cell")),
        check_vma=False,
    )
```

```python
import functools

import jax
import jax.numpy as jnp
from jax import lax
from jax.experimental import pallas as pl
from jax.experimental.pallas import tpu as pltpu
from jax.sharding import PartitionSpec as P

CAM_TILE = 64
REACH = 2
SPAN = 2 * REACH + 1
ORDER = sorted(range(-REACH, REACH + 1), key=abs)
LANES = 128
ROWS = 8
PACK = 32
NONE = -(1 << 20)
MESH = pl.DeviceIdType.MESH
F32 = jnp.float32
BF16 = jnp.bfloat16
I32 = jnp.int32


def round_up(value, step):
    return (value + step - 1) // step * step


def kernel(
    cells,
    grps,
    guess_hbm,
    right_hbm,
    blocks_hbm,
    inverse_hbm,
    jac_hbm,
    pattern_hbm,
    load_hbm,
    solution_ref,
    residual_ref,
    pattern,
    load,
    guess,
    right,
    blocks,
    inverse,
    jac,
    fields,
    keys,
    slot_send,
    slot_recv,
    scalar_send,
    scalar_recv,
    choose_slots,
    choose_field,
    choose_window,
    local_sem,
    jac_sem,
    field_send_sem,
    field_recv_sem,
    key_send_sem,
    key_recv_sem,
    slot_send_sem,
    slot_recv_sem,
    scalar_sem,
):
    params, cameras = guess.shape
    slots, rows_wide, points_wide = jac.shape
    tiles = cameras // CAM_TILE
    pairs = cameras // LANES
    coords = inverse.shape[0]
    point_tiles = inverse.shape[2] // LANES
    full = rows_wide // LANES
    slot_rows_sent = round_up(full * slots + slots // 2, 4)
    field_rows = full * tiles + tiles // 2
    field_rows_sent = round_up(field_rows, ROWS)
    field_pack = fields.shape[2]
    near_count = SPAN * grps
    close_count = 3 * grps
    devices = cells * grps
    cell = lax.axis_index("cell")
    grp = lax.axis_index("grp")

    def near(delta, turn):
        return (lax.rem(cell + delta + cells, cells), lax.rem(grp + turn + grps, grps))

    def slot_index(delta, turn):
        return ORDER.index(delta) * grps + turn % grps

    peers = sorted(
        [(d, t) for d in ORDER for t in range(grps) if (d, t) != (0, 0)],
        key=lambda peer: ((abs(peer[0]) + REACH) % (REACH + 1), -peer[1]),
    )
    first_wave = [(d, t) for d, t in peers if d == 0 or t == 0]
    second_wave = [(d, t) for d, t in peers if d != 0 and t != 0]
    key_index = {(0, 0): 0}
    for delta, turn in first_wave + second_wave:
        key_index[(delta, turn)] = len(key_index)

    turned = [lax.rem(grp + turn, grps) for turn in range(grps)]

    def everyone(act):
        for turn in range(1, grps):
            act(turn - 1, (cell, turned[turn]))

        def one_cell(delta, carry):
            other = lax.rem(cell + delta, cells)
            for turn in range(grps):
                act(delta * grps + (turn - 1), (other, turned[turn]))
            return carry

        lax.fori_loop(1, cells, one_cell, 0)

    barrier = pltpu.get_barrier_semaphore()

    def greet(index, device):
        pl.semaphore_signal(barrier, inc=1, device_id=device, device_id_type=MESH)

    if cells // 2 <= 2 * REACH:
        greeted = len(first_wave)
        for delta, turn in first_wave:
            greet(0, near(delta, turn))
    else:
        greeted = devices - 1
        everyone(greet)

    local = [
        pltpu.make_async_copy(src, dst, local_sem.at[i])
        for i, (src, dst) in enumerate(
            (
                (guess_hbm, guess),
                (pattern_hbm, pattern),
                (load_hbm, load),
                (blocks_hbm, blocks),
                (right_hbm, right),
                (inverse_hbm, inverse),
            )
        )
    ]
    jac_copies = [
        pltpu.make_async_copy(jac_hbm.at[s], jac.at[s], jac_sem.at[s]) for s in range(slots)
    ]
    for copy in local:
        copy.start()
    for copy in jac_copies:
        copy.start()

    def iota(shape, axis):
        return lax.broadcasted_iota(I32, shape, axis)

    def steps(value, width, count):
        return sum((value >= width * j).astype(I32) for j in range(1, count + 1))

    lane8 = iota((ROWS, LANES), 1)
    row8 = iota((ROWS, LANES), 0)
    low8 = lane8 < CAM_TILE
    low1 = iota((1, LANES), 1) < CAM_TILE
    even8 = lax.bitwise_and(row8, 1) == 0

    fields[:, :, field_rows_sent:, :] = jnp.zeros(
        (fields.shape[0], 3, field_pack - field_rows_sent, LANES), BF16
    )
    slot_recv[:, :, slot_rows_sent:, :] = jnp.zeros(
        (3, near_count, PACK - slot_rows_sent, LANES), BF16
    )

    pick_row = iota((field_pack, LANES), 0)
    pick_chunk = steps(pick_row, tiles, full)
    pick_tile = pick_row - pick_chunk * tiles
    pick_tail = pick_chunk == full
    source_low = 16 * pick_tile + 2 * pick_chunk
    other_tile = jnp.where(pick_tail, pick_tile + tiles // 2, pick_tile)
    flipped = other_tile + 1 - 2 * lax.bitwise_and(other_tile, 1)
    source_high = 16 * flipped + jnp.where(pick_tail, 2 * full, 2 * pick_chunk + 1)
    unused = pick_row >= field_rows
    source_low = jnp.where(unused, -1, source_low)
    source_high = jnp.where(unused, -1, source_high)
    picked_width = 16 * tiles
    lane_pick = iota((field_pack, LANES), 1)

    def one_hot(source):
        parts = [
            (source == lane_pick + LANES * j).astype(F32)
            for j in range(round_up(picked_width, LANES) // LANES)
        ]
        return jnp.concatenate(parts, axis=1)[:, :picked_width].astype(BF16)

    spread = jnp.concatenate([one_hot(source_low), one_hot(source_high)], axis=0)

    def to_rows(field):
        tall = jnp.concatenate([field, jnp.zeros((16 - params, cameras), F32)], axis=0)
        parts = []
        for i in range(pairs):
            block = tall[:, i * LANES : (i + 1) * LANES]
            parts += [block.astype(BF16), pltpu.roll(block, CAM_TILE, 1).astype(BF16)]
        both = jnp.dot(spread, jnp.concatenate(parts, axis=0), preferred_element_type=F32)
        low = lane_pick < CAM_TILE
        picked = jnp.where(low, both[:field_pack], both[field_pack:])
        return picked[:field_rows_sent].astype(BF16)

    def put_field(f, field):
        fields[f, 2, :field_rows_sent] = to_rows(field)

    def field_copies(f):
        return [
            pltpu.make_async_remote_copy(
                src_ref=fields.at[f, 2, pl.ds(0, field_rows_sent)],
                dst_ref=fields.at[f, side, pl.ds(0, field_rows_sent)],
                send_sem=field_send_sem.at[f],
                recv_sem=field_recv_sem.at[f],
                device_id=near(delta, 0),
                device_id_type=MESH,
            )
            for side, delta in ((0, 1), (1, -1))
        ]

    def wait_bytes(ref, sem):
        pltpu.make_async_copy(ref, ref, sem).wait()

    def field_bytes(f, sem):
        wait_bytes(fields.at[f, pl.ds(0, 2), pl.ds(0, field_rows_sent)], sem.at[f])

    local[0].wait()
    put_field(0, guess[...])

    local[1].wait()
    local[2].wait()
    live = [s < load[0] for s in range(slots)]
    ids = [pattern[0, s] for s in range(slots)]
    point_ids = [pattern[1, s] for s in range(slots)]
    live_rows = jnp.zeros((ROWS, LANES), I32)
    id_rows = jnp.full((ROWS, LANES), NONE, I32)
    point_rows = jnp.full((ROWS, LANES), -1, I32)
    first_rows = jnp.zeros((ROWS, LANES), F32)
    for s in range(slots):
        here = row8 == s
        id_rows = jnp.where(here, jnp.where(live[s], 8 * ids[s], NONE), id_rows)
        point_rows = jnp.where(here, point_ids[s], point_rows)
        live_rows = jnp.where(here, jnp.where(live[s], 1, 0), live_rows)
        first = live[s]
        for u in range(s):
            same = jnp.logical_and(live[u], point_ids[u] == point_ids[s])
            first = jnp.logical_and(first, jnp.logical_not(same))
        first_rows = jnp.where(here, jnp.where(first, 1.0, 0.0), first_rows)
    live8 = live_rows > 0
    shared = [
        jnp.logical_and(point_rows == point_ids[s], jnp.where(live[s], 1, 0) > 0)
        for s in range(slots)
    ]

    key_lane = lax.bitwise_and(iota((2, LANES), 1), PACK - 1)
    key_chunk = steps(key_lane, slots, full)
    key_slot = key_lane - slots * key_chunk
    key_row = iota((2, LANES), 0)
    key_tail = jnp.logical_and(key_chunk == full, key_slot < slots // 2)
    own_key = jnp.full((2, LANES), NONE, I32)
    for s in range(slots):
        code = jnp.where(live[s], 8 * ids[s], NONE)
        head = jnp.logical_and(jnp.logical_and(key_chunk < full, key_slot == s), key_row == 0)
        tail_row, tail_slot = divmod(s, slots // 2)
        tail = jnp.logical_and(
            jnp.logical_and(key_tail, key_slot == tail_slot), key_row == tail_row
        )
        own_key = jnp.where(head, code + key_chunk, own_key)
        own_key = jnp.where(tail, code + full + tail_row, own_key)
    keys[0] = own_key

    row_keys = [id_rows + b for b in range(full + 2)]

    window_lane = iota((1, LANES), 1)
    window_parts = [[], []]
    window_width = 3 * field_pack
    for group in range(round_up(window_width, LANES) // LANES):
        position = window_lane + LANES * group
        place = steps(position, field_pack, 2)
        side = jnp.where(place == 0, 0, jnp.where(place == 1, 2, 1))
        row = position - place * field_pack
        chunk = steps(row, tiles, full)
        tile = side * tiles + row - chunk * tiles
        off = row >= field_rows
        tail = jnp.logical_and(chunk == full, jnp.logical_not(off))
        window_parts[0].append(jnp.where(off, -1, 8 * tile + chunk))
        window_parts[1].append(jnp.where(tail, 8 * (tile + tiles // 2) + full + 1, -1))
    window_low = window_parts[0]
    window_high = window_parts[1]

    def matches(low_keys, high_keys):
        parts = []
        for b in range(full + 2):
            found = low_keys if b <= full else high_keys
            parts.append(
                jnp.concatenate([(key == row_keys[b]).astype(F32) for key in found], axis=1)
            )
        return jnp.concatenate(parts, axis=0).astype(BF16)

    choose_window[...] = matches(window_low, window_high)[:, :window_width]

    def slot_fields(chosen, rows):
        found = jnp.dot(chosen, rows, preferred_element_type=F32)
        parts = [found[b * ROWS : (b + 1) * ROWS] for b in range(full + 2)]
        tail = parts[full] + pltpu.roll(parts[full + 1], CAM_TILE, 1)
        return jnp.concatenate(parts[:full] + [tail], axis=1)[:, :rows_wide]

    def window_slots(f):
        return slot_fields(choose_window[...], fields[f].reshape(window_width, LANES))

    def block_product(field):
        total = blocks[0] * field[0:1, :]
        for k in range(1, params):
            total = total + blocks[k] * field[k : k + 1, :]
        return total

    local[3].wait()
    row_wide = iota((params, cameras), 0)
    diagonal = blocks[0]
    for k in range(1, params):
        diagonal = jnp.where(row_wide == k, blocks[k], diagonal)
    scale = 1.0 / diagonal
    local[4].wait()
    residual0 = right[...] - block_product(guess[...])
    put_field(1, residual0 * scale)
    put_field(2, scale)
    local[5].wait()
    inverse_rows = []
    for j in range(coords):
        for i in range(coords):
            picked = jnp.zeros((ROWS, LANES), F32)
            for q in range(point_tiles):
                picked = jnp.where(
                    point_rows == q, inverse[j, i : i + 1, q * LANES : (q + 1) * LANES], picked
                )
            inverse_rows.append(picked)

    for copy in jac_copies:
        copy.wait()
    pl.semaphore_wait(barrier, greeted)

    for copy in field_copies(0):
        copy.start()

    def send_keys(wave, sem):
        for delta, turn in wave:
            pltpu.make_async_remote_copy(
                src_ref=keys.at[0],
                dst_ref=keys.at[key_index[(-delta, -turn % grps)]],
                send_sem=key_send_sem.at[sem],
                recv_sem=key_recv_sem.at[sem],
                device_id=near(delta, turn),
                device_id_type=MESH,
            ).start()

    first_keys = pl.ds(1, len(first_wave))
    second_keys = pl.ds(1 + len(first_wave), len(second_wave))
    send_keys(first_wave, 0)
    for f in (1, 2):
        for copy in field_copies(f):
            copy.start()

    def slot_rows(values):
        values = jnp.where(live_wide, values, 0.0)
        sums = jnp.zeros((ROWS, points_wide), F32)
        for s in range(slots):
            spread_row = jnp.where(shared_wide[s], values[s : s + 1, :], 0.0)
            sums = sums + jnp.dot(spread_row.astype(BF16), jac[s], preferred_element_type=F32)
        solved = []
        for j in range(coords):
            total = inverse_rows[j * coords] * sums[:, :LANES]
            for i in range(1, coords):
                total = total + inverse_rows[j * coords + i] * sums[:, i * LANES : (i + 1) * LANES]
            solved.append(total)
        solved = jnp.concatenate(solved, axis=1).astype(BF16).astype(F32)
        return sums, solved

    def slot_message(solved):
        parts = [jnp.zeros((ROWS, LANES), F32) for _ in range(PACK // ROWS)]
        tails = []
        for s in range(slots):
            row = jnp.broadcast_to(solved[s : s + 1, :], (ROWS, points_wide)).astype(BF16)
            product = lax.dot_general(
                row, jac[s], (((1,), (1,)), ((), ())), preferred_element_type=F32
            )
            product = jnp.where(live[s], product, 0.0)
            for b in range(full):
                at, inside = divmod(b * slots + s, ROWS)
                parts[at] = jnp.where(
                    row8 == inside, product[:, b * LANES : (b + 1) * LANES], parts[at]
                )
            tails.append(product[:, full * LANES :])
        for i in range(slots // 2):
            at, inside = divmod(full * slots + i, ROWS)
            both = jnp.concatenate([tails[i], tails[i + slots // 2]], axis=1)
            parts[at] = jnp.where(row8 == inside, both, parts[at])
        return jnp.concatenate(parts, axis=0).astype(BF16)

    def energy_of(sums, solved):
        energy = sums * solved
        lanes = energy[:, :LANES]
        for i in range(1, coords):
            lanes = lanes + energy[:, i * LANES : (i + 1) * LANES]
        return jnp.sum(lanes * first_rows, axis=0, keepdims=True)

    live_wide = jnp.concatenate([live8] * (full + 1), axis=1)[:, :rows_wide]
    shared_wide = [
        jnp.concatenate([shared[s]] * (full + 1), axis=1)[:, :rows_wide] for s in range(slots)
    ]

    def send_slots(turn_no, message, reach):
        slot_send[turn_no] = message
        slot_recv[turn_no, 0] = message
        for delta, turn in peers:
            if abs(delta) <= reach:
                pltpu.make_async_remote_copy(
                    src_ref=slot_send.at[turn_no, pl.ds(0, slot_rows_sent)],
                    dst_ref=slot_recv.at[
                        turn_no, slot_index(-delta, -turn), pl.ds(0, slot_rows_sent)
                    ],
                    send_sem=slot_send_sem.at[turn_no],
                    recv_sem=slot_recv_sem.at[turn_no],
                    device_id=near(delta, turn),
                    device_id_type=MESH,
                ).start()

    def wait_slots(turn_no, count, sem):
        wait_bytes(
            slot_recv.at[turn_no, pl.ds(1, count - 1), pl.ds(0, slot_rows_sent)], sem.at[turn_no]
        )

    def received(turn_no, count):
        return slot_recv[turn_no, :count].reshape(count * PACK, LANES)

    def own_back(turn_no, count):
        width = count * PACK
        found = jnp.dot(
            choose_field[:, :width], received(turn_no, count), preferred_element_type=F32
        )
        parts = []
        for i in range(pairs):
            first = found[32 * i : 32 * i + 16]
            second = found[32 * i + 16 : 32 * i + 32]
            first_turned = pltpu.roll(first, CAM_TILE, 1)
            second_turned = pltpu.roll(second, CAM_TILE, 1)
            top = jnp.where(
                low8,
                jnp.where(even8, first[:ROWS], first_turned[:ROWS]),
                jnp.where(even8, second_turned[:ROWS], second[:ROWS]),
            )
            last = jnp.where(
                low1,
                first[ROWS : ROWS + 1] + first_turned[ROWS + 1 : ROWS + 2],
                second_turned[ROWS : ROWS + 1] + second[ROWS + 1 : ROWS + 2],
            )
            parts.append(jnp.concatenate([top, last], axis=0))
        return jnp.concatenate(parts, axis=1)

    field_bytes(0, field_recv_sem)
    wait_bytes(keys.at[first_keys], key_recv_sem.at[0])
    send_keys(second_wave, 1)
    _, solved = slot_rows(window_slots(0))
    send_slots(0, slot_message(solved), REACH)

    wait_bytes(keys.at[second_keys], key_recv_sem.at[1])
    lows, highs = [], []
    place_lane = lax.shift_right_logical(window_lane, 5)
    per_group = LANES // PACK
    order = [(delta, turn) for delta in ORDER for turn in range(grps)]
    for group in range(near_count // per_group):
        low = jnp.full((1, LANES), NONE, I32)
        high = jnp.full((1, LANES), NONE, I32)
        for j in range(per_group):
            delta, turn = order[group * per_group + j]
            key = keys[key_index[(delta, turn)]] + 8 * tiles * delta
            low = jnp.where(place_lane == j, key[0:1], low)
            high = jnp.where(place_lane == j, key[1:2], high)
        lows.append(low)
        highs.append(high)
    choose_slots[...] = matches(lows, highs)
    half_row = lax.shift_right_logical(row8, 1)
    mixed = [jnp.where(row8 == 0, low, high) for low, high in zip(lows, highs)]
    for t in range(tiles):
        base = 8 * (tiles + t)
        top = jnp.concatenate([(low == base + half_row).astype(F32) for low in lows], axis=1)
        tail_key = jnp.where(row8 < 2, base + full + row8, -1)
        tail = jnp.concatenate([(mix == tail_key).astype(F32) for mix in mixed], axis=1)
        choose_field[16 * t : 16 * (t + 1)] = jnp.concatenate([top, tail], axis=0).astype(BF16)
    for f in (1, 2):
        field_bytes(f, field_recv_sem)
    start_slots = window_slots(1)
    scale_slots = window_slots(2)

    wait_slots(0, near_count, slot_recv_sem)
    back = slot_fields(choose_slots[...], received(0, near_count))
    own_found = own_back(0, near_count)
    direction_slots = start_slots + scale_slots * back
    _, solved = slot_rows(direction_slots)
    residual0 = residual0 + own_found
    direction = residual0 * scale
    product1 = block_product(direction)
    put_field(3, (product1 - diagonal * direction) * scale)
    for copy in field_copies(3):
        copy.start()
    field_bytes(1, field_send_sem)
    send_slots(1, slot_message(solved), REACH)
    field_bytes(3, field_recv_sem)
    change_slots = window_slots(3)

    wait_slots(1, near_count, slot_recv_sem)
    back = slot_fields(choose_slots[...], received(1, near_count))
    own_found = own_back(1, near_count)
    sums, solved = slot_rows(scale_slots * back - change_slots)
    send_slots(2, slot_message(solved), 1)
    field_bytes(2, field_send_sem)
    energy = energy_of(sums, solved)
    image1 = product1 - own_found
    trial = residual0 - image1
    shaped = trial * scale
    product2 = block_product(shaped)

    def lane_sum(field):
        total = field[:, :LANES]
        for i in range(1, pairs):
            total = total + field[:, i * LANES : (i + 1) * LANES]
        return jnp.sum(total, axis=0, keepdims=True) * (1.0 / grps)

    sums = jnp.zeros((ROWS, LANES), F32)
    for i, value in enumerate(
        (
            lane_sum(residual0 * direction),
            lane_sum(direction * image1),
            lane_sum(residual0 * shaped),
            lane_sum(trial * shaped),
            lane_sum(image1 * shaped),
            lane_sum(shaped * product2) - energy,
        )
    ):
        sums = jnp.where(row8 == i, value, sums)
    sums = jnp.sum(sums, axis=1, keepdims=True)
    own_sums = jnp.sum(jnp.where(row8 == lane8, sums, 0.0), axis=0, keepdims=True)
    scalar_send[...] = own_sums

    def send_scalars(index, device):
        pltpu.make_async_remote_copy(
            src_ref=scalar_send,
            dst_ref=scalar_recv.at[index],
            send_sem=scalar_sem.at[0],
            recv_sem=scalar_sem.at[1],
            device_id=device,
            device_id_type=MESH,
        ).start()

    everyone(send_scalars)

    wait_slots(2, close_count, slot_recv_sem)
    image2 = product2 - own_back(2, close_count)
    wait_bytes(scalar_recv, scalar_sem.at[1])
    totals = own_sums + jnp.sum(scalar_recv[...], axis=0)
    rz0, curve1, cross, trial_rz, mixed_sum, curve_w = [totals[:, i : i + 1] for i in range(6)]
    step1 = rz0 / curve1
    short = 1.0 - step1
    rz1 = short * short * rz0 + 2.0 * short * step1 * cross + step1 * step1 * trial_rz
    keep = short + rz1 / rz0
    curve2 = keep * keep * curve1 + 2.0 * keep * step1 * mixed_sum + step1 * step1 * curve_w
    step2 = rz1 / curve2
    near_part = step1 + step2 * keep
    far_part = step2 * step1
    solution_ref[...] = guess[...] + near_part * direction + far_part * shaped
    residual_ref[...] = residual0 - near_part * image1 - far_part * image2

    wait_bytes(scalar_recv, scalar_sem.at[0])
    for f in (0, 3):
        field_bytes(f, field_send_sem)
    wait_bytes(keys.at[first_keys], key_send_sem.at[0])
    wait_bytes(keys.at[second_keys], key_send_sem.at[1])
    for turn_no, count in enumerate((near_count, near_count, close_count)):
        wait_slots(turn_no, count, slot_send_sem)


def finish_kernel(first, second, solution_ref, residual_ref):
    solution_ref[...] = first[...]
    residual_ref[...] = second[...]


def finish(first, second):
    vmem = pl.BlockSpec(memory_space=pltpu.VMEM)
    shape = jax.ShapeDtypeStruct(first.shape, first.dtype)
    return pl.pallas_call(
        finish_kernel, out_shape=(shape, shape), in_specs=[vmem] * 2, out_specs=(vmem, vmem)
    )(*[pltpu.with_memory_space_constraint(x, pltpu.VMEM) for x in (first, second)])


def per_device(
    cells, grps, initial_guess, right_side, camera_blocks, point_inverse, jacobian_tiles, tile_pattern, cell_load
):
    params, cameras = initial_guess.shape
    slots, rows_wide, points_wide = jacobian_tiles.shape
    near = SPAN * grps
    tiles = cameras // CAM_TILE
    full = rows_wide // LANES
    field_pack = round_up(full * tiles + tiles // 2, 64)
    hbm = pl.BlockSpec(memory_space=pltpu.HBM)
    vmem = pl.BlockSpec(memory_space=pltpu.VMEM)
    dma = pltpu.SemaphoreType.DMA
    field = pltpu.VMEM((params, cameras), F32)
    first, second = pl.pallas_call(
        functools.partial(kernel, cells, grps),
        out_shape=(field, field),
        in_specs=[hbm] * 7,
        out_specs=(vmem, vmem),
        scratch_shapes=[
            pltpu.SMEM((2, slots), I32),
            pltpu.SMEM((1,), I32),
            pltpu.VMEM((params, cameras), F32),
            pltpu.VMEM((params, cameras), F32),
            pltpu.VMEM(camera_blocks.shape, F32),
            pltpu.VMEM(point_inverse.shape, F32),
            pltpu.VMEM(jacobian_tiles.shape, BF16),
            pltpu.VMEM((4, 3, field_pack, LANES), BF16),
            pltpu.VMEM((near, 2, LANES), I32),
            pltpu.VMEM((3, PACK, LANES), BF16),
            pltpu.VMEM((3, near, PACK, LANES), BF16),
            pltpu.VMEM((1, LANES), F32),
            pltpu.VMEM((cells * grps - 1, 1, LANES), F32),
            pltpu.VMEM((ROWS * (full + 2), near * PACK), BF16),
            pltpu.VMEM((16 * tiles, near * PACK), BF16),
            pltpu.VMEM((ROWS * (full + 2), 3 * field_pack), BF16),
            dma((6,)),
            dma((slots,)),
            dma((4,)),
            dma((4,)),
            dma((2,)),
            dma((2,)),
            dma((3,)),
            dma((3,)),
            dma((2,)),
        ],
        compiler_params=pltpu.CompilerParams(collective_id=0, has_side_effects=True),
    )(initial_guess, right_side, camera_blocks, point_inverse, jacobian_tiles, tile_pattern.T, cell_load)
    return finish(first, second)


def solution(mesh):
    placed = (
        P(None, "cell"),
        P(None, "cell"),
        P(None, None, "cell"),
        P(None, None, ("cell", "grp")),
        P(("cell", "grp"), None, None),
        P(("cell", "grp"), None),
        P("cell"),
    )
    return jax.shard_map(
        functools.partial(per_device, mesh.shape["cell"], mesh.shape["grp"]),
        mesh=mesh,
        in_specs=placed,
        out_specs=(P(None, "cell"), P(None, "cell")),
        check_vma=False,
    )
```

```python
import functools

import jax
import jax.numpy as jnp
from jax import lax
from jax.experimental import pallas as pl
from jax.experimental.pallas import tpu as pltpu
from jax.sharding import PartitionSpec as P

CAM_TILE = 64
REACH = 2
SPAN = 2 * REACH + 1
ORDER = sorted(range(-REACH, REACH + 1), key=abs)
LANES = 128
ROWS = 8
PACK = 32
NONE = -(1 << 20)
MESH = pl.DeviceIdType.MESH
F32 = jnp.float32
BF16 = jnp.bfloat16
I32 = jnp.int32


def round_up(value, step):
    return (value + step - 1) // step * step


def kernel(
    cells,
    grps,
    guess_hbm,
    right_hbm,
    blocks_hbm,
    inverse_hbm,
    jac_hbm,
    pattern_hbm,
    load_hbm,
    solution_ref,
    residual_ref,
    pattern,
    load,
    guess,
    right,
    blocks,
    inverse,
    jac,
    jac_turned,
    fields,
    keys,
    slot_send,
    slot_recv,
    scalar_send,
    scalar_recv,
    choose_slots,
    choose_field,
    choose_window,
    local_sem,
    jac_sem,
    field_send_sem,
    field_recv_sem,
    key_send_sem,
    key_recv_sem,
    slot_send_sem,
    slot_recv_sem,
    scalar_sem,
):
    params, cameras = guess.shape
    slots, rows_wide, points_wide = jac.shape
    tiles = cameras // CAM_TILE
    pairs = cameras // LANES
    coords = inverse.shape[0]
    point_tiles = inverse.shape[2] // LANES
    full = rows_wide // LANES
    slot_rows_sent = round_up(full * slots + slots // 2, 4)
    field_rows = full * tiles + tiles // 2
    field_rows_sent = round_up(field_rows, ROWS)
    field_pack = fields.shape[2]
    near_count = SPAN * grps
    close_count = 3 * grps
    devices = cells * grps
    cell = lax.axis_index("cell")
    grp = lax.axis_index("grp")

    def near(delta, turn):
        return (lax.rem(cell + delta + cells, cells), lax.rem(grp + turn + grps, grps))

    def slot_index(delta, turn):
        return ORDER.index(delta) * grps + turn % grps

    peers = sorted(
        [(d, t) for d in ORDER for t in range(grps) if (d, t) != (0, 0)],
        key=lambda peer: ((abs(peer[0]) + REACH) % (REACH + 1), -peer[1]),
    )
    first_wave = [(d, t) for d, t in peers if d == 0 or t == 0]
    second_wave = [(d, t) for d, t in peers if d != 0 and t != 0]
    key_index = {(0, 0): 0}
    for delta, turn in first_wave + second_wave:
        key_index[(delta, turn)] = len(key_index)

    turned = [lax.rem(grp + turn, grps) for turn in range(grps)]

    def everyone(act):
        for turn in range(1, grps):
            act(turn - 1, (cell, turned[turn]))

        def one_cell(delta, carry):
            other = lax.rem(cell + delta, cells)
            for turn in range(grps):
                act(delta * grps + (turn - 1), (other, turned[turn]))
            return carry

        lax.fori_loop(1, cells, one_cell, 0)

    barrier = pltpu.get_barrier_semaphore()

    def greet(index, device):
        pl.semaphore_signal(barrier, inc=1, device_id=device, device_id_type=MESH)

    if cells // 2 <= 2 * REACH:
        greeted = len(first_wave)
        for delta, turn in first_wave:
            greet(0, near(delta, turn))
    else:
        greeted = devices - 1
        everyone(greet)

    local = [
        pltpu.make_async_copy(src, dst, local_sem.at[i])
        for i, (src, dst) in enumerate(
            (
                (guess_hbm, guess),
                (pattern_hbm, pattern),
                (load_hbm, load),
                (blocks_hbm, blocks),
                (right_hbm, right),
                (inverse_hbm, inverse),
            )
        )
    ]
    jac_copies = [
        pltpu.make_async_copy(jac_hbm.at[s], jac.at[s], jac_sem.at[s]) for s in range(slots)
    ]
    for copy in local:
        copy.start()
    for copy in jac_copies:
        copy.start()

    def iota(shape, axis):
        return lax.broadcasted_iota(I32, shape, axis)

    def steps(value, width, count):
        return sum((value >= width * j).astype(I32) for j in range(1, count + 1))

    lane8 = iota((ROWS, LANES), 1)
    row8 = iota((ROWS, LANES), 0)
    low8 = lane8 < CAM_TILE
    low1 = iota((1, LANES), 1) < CAM_TILE
    even8 = lax.bitwise_and(row8, 1) == 0

    fields[:, :, field_rows_sent:, :] = jnp.zeros(
        (fields.shape[0], 3, field_pack - field_rows_sent, LANES), BF16
    )
    slot_recv[:, :, slot_rows_sent:, :] = jnp.zeros(
        (3, near_count, PACK - slot_rows_sent, LANES), BF16
    )

    pick_row = iota((field_pack, LANES), 0)
    pick_chunk = steps(pick_row, tiles, full)
    pick_tile = pick_row - pick_chunk * tiles
    pick_tail = pick_chunk == full
    source_low = 16 * pick_tile + 2 * pick_chunk
    other_tile = jnp.where(pick_tail, pick_tile + tiles // 2, pick_tile)
    flipped = other_tile + 1 - 2 * lax.bitwise_and(other_tile, 1)
    source_high = 16 * flipped + jnp.where(pick_tail, 2 * full, 2 * pick_chunk + 1)
    unused = pick_row >= field_rows
    source_low = jnp.where(unused, -1, source_low)
    source_high = jnp.where(unused, -1, source_high)
    picked_width = 16 * tiles
    lane_pick = iota((field_pack, LANES), 1)

    def one_hot(source):
        parts = [
            (source == lane_pick + LANES * j).astype(F32)
            for j in range(round_up(picked_width, LANES) // LANES)
        ]
        return jnp.concatenate(parts, axis=1)[:, :picked_width].astype(BF16)

    spread = jnp.concatenate([one_hot(source_low), one_hot(source_high)], axis=0)

    def to_rows(field):
        tall = jnp.concatenate([field, jnp.zeros((16 - params, cameras), F32)], axis=0)
        parts = []
        for i in range(pairs):
            block = tall[:, i * LANES : (i + 1) * LANES]
            parts += [block.astype(BF16), pltpu.roll(block, CAM_TILE, 1).astype(BF16)]
        both = jnp.dot(spread, jnp.concatenate(parts, axis=0), preferred_element_type=F32)
        low = lane_pick < CAM_TILE
        picked = jnp.where(low, both[:field_pack], both[field_pack:])
        return picked[:field_rows_sent].astype(BF16)

    def put_field(f, field):
        fields[f, 2, :field_rows_sent] = to_rows(field)

    def field_copies(f):
        return [
            pltpu.make_async_remote_copy(
                src_ref=fields.at[f, 2, pl.ds(0, field_rows_sent)],
                dst_ref=fields.at[f, side, pl.ds(0, field_rows_sent)],
                send_sem=field_send_sem.at[f],
                recv_sem=field_recv_sem.at[f],
                device_id=near(delta, 0),
                device_id_type=MESH,
            )
            for side, delta in ((0, 1), (1, -1))
        ]

    def wait_bytes(ref, sem):
        pltpu.make_async_copy(ref, ref, sem).wait()

    def field_bytes(f, sem):
        wait_bytes(fields.at[f, pl.ds(0, 2), pl.ds(0, field_rows_sent)], sem.at[f])

    local[0].wait()
    put_field(0, guess[...])

    local[1].wait()
    local[2].wait()
    live = [s < load[0] for s in range(slots)]
    ids = [pattern[0, s] for s in range(slots)]
    point_ids = [pattern[1, s] for s in range(slots)]
    live_rows = jnp.zeros((ROWS, LANES), I32)
    id_rows = jnp.full((ROWS, LANES), NONE, I32)
    point_rows = jnp.full((ROWS, LANES), -1, I32)
    first_rows = jnp.zeros((ROWS, LANES), F32)
    for s in range(slots):
        here = row8 == s
        id_rows = jnp.where(here, jnp.where(live[s], 8 * ids[s], NONE), id_rows)
        point_rows = jnp.where(here, point_ids[s], point_rows)
        live_rows = jnp.where(here, jnp.where(live[s], 1, 0), live_rows)
        first = live[s]
        for u in range(s):
            same = jnp.logical_and(live[u], point_ids[u] == point_ids[s])
            first = jnp.logical_and(first, jnp.logical_not(same))
        first_rows = jnp.where(here, jnp.where(first, 1.0, 0.0), first_rows)
    live8 = live_rows > 0
    shared = [
        jnp.logical_and(point_rows == point_ids[s], jnp.where(live[s], 1, 0) > 0)
        for s in range(slots)
    ]

    key_lane = lax.bitwise_and(iota((2, LANES), 1), PACK - 1)
    key_chunk = steps(key_lane, slots, full)
    key_slot = key_lane - slots * key_chunk
    key_row = iota((2, LANES), 0)
    key_tail = jnp.logical_and(key_chunk == full, key_slot < slots // 2)
    own_key = jnp.full((2, LANES), NONE, I32)
    for s in range(slots):
        code = jnp.where(live[s], 8 * ids[s], NONE)
        head = jnp.logical_and(jnp.logical_and(key_chunk < full, key_slot == s), key_row == 0)
        tail_row, tail_slot = divmod(s, slots // 2)
        tail = jnp.logical_and(
            jnp.logical_and(key_tail, key_slot == tail_slot), key_row == tail_row
        )
        own_key = jnp.where(head, code + key_chunk, own_key)
        own_key = jnp.where(tail, code + full + tail_row, own_key)
    keys[0] = own_key

    row_keys = [id_rows + b for b in range(full + 2)]

    window_lane = iota((1, LANES), 1)
    window_parts = [[], []]
    window_width = 3 * field_pack
    for group in range(round_up(window_width, LANES) // LANES):
        position = window_lane + LANES * group
        place = steps(position, field_pack, 2)
        side = jnp.where(place == 0, 0, jnp.where(place == 1, 2, 1))
        row = position - place * field_pack
        chunk = steps(row, tiles, full)
        tile = side * tiles + row - chunk * tiles
        off = row >= field_rows
        tail = jnp.logical_and(chunk == full, jnp.logical_not(off))
        window_parts[0].append(jnp.where(off, -1, 8 * tile + chunk))
        window_parts[1].append(jnp.where(tail, 8 * (tile + tiles // 2) + full + 1, -1))
    window_low = window_parts[0]
    window_high = window_parts[1]

    def matches(low_keys, high_keys):
        parts = []
        for b in range(full + 2):
            found = low_keys if b <= full else high_keys
            parts.append(
                jnp.concatenate([(key == row_keys[b]).astype(F32) for key in found], axis=1)
            )
        return jnp.concatenate(parts, axis=0).astype(BF16)

    choose_window[...] = matches(window_low, window_high)[:, :window_width]

    def slot_fields(chosen, rows):
        found = jnp.dot(chosen, rows, preferred_element_type=F32)
        parts = [found[b * ROWS : (b + 1) * ROWS] for b in range(full + 2)]
        tail = parts[full] + pltpu.roll(parts[full + 1], CAM_TILE, 1)
        return jnp.concatenate(parts[:full] + [tail], axis=1)[:, :rows_wide]

    def window_slots(f):
        return slot_fields(choose_window[...], fields[f].reshape(window_width, LANES))

    def block_product(field):
        total = blocks[0] * field[0:1, :]
        for k in range(1, params):
            total = total + blocks[k] * field[k : k + 1, :]
        return total

    local[3].wait()
    row_wide = iota((params, cameras), 0)
    diagonal = blocks[0]
    for k in range(1, params):
        diagonal = jnp.where(row_wide == k, blocks[k], diagonal)
    scale = 1.0 / diagonal
    local[4].wait()
    residual0 = right[...] - block_product(guess[...])
    put_field(1, residual0 * scale)
    put_field(2, scale)
    local[5].wait()
    inverse_rows = []
    for j in range(coords):
        for i in range(coords):
            picked = jnp.zeros((ROWS, LANES), F32)
            for q in range(point_tiles):
                picked = jnp.where(
                    point_rows == q, inverse[j, i : i + 1, q * LANES : (q + 1) * LANES], picked
                )
            inverse_rows.append(picked)

    for copy in jac_copies:
        copy.wait()
    pl.semaphore_wait(barrier, greeted)

    for copy in field_copies(0):
        copy.start()

    def send_keys(wave, sem):
        for delta, turn in wave:
            pltpu.make_async_remote_copy(
                src_ref=keys.at[0],
                dst_ref=keys.at[key_index[(-delta, -turn % grps)]],
                send_sem=key_send_sem.at[sem],
                recv_sem=key_recv_sem.at[sem],
                device_id=near(delta, turn),
                device_id_type=MESH,
            ).start()

    first_keys = pl.ds(1, len(first_wave))
    second_keys = pl.ds(1 + len(first_wave), len(second_wave))
    send_keys(first_wave, 0)
    for f in (1, 2):
        for copy in field_copies(f):
            copy.start()
    for s in range(slots):
        jac_turned[s] = jac[s].T

    def slot_rows(values):
        values = jnp.where(live_wide, values, 0.0)
        sums = jnp.zeros((ROWS, points_wide), F32)
        for s in range(slots):
            spread_row = jnp.where(shared_wide[s], values[s : s + 1, :], 0.0)
            sums = sums + jnp.dot(spread_row.astype(BF16), jac[s], preferred_element_type=F32)
        solved = []
        for j in range(coords):
            total = inverse_rows[j * coords] * sums[:, :LANES]
            for i in range(1, coords):
                total = total + inverse_rows[j * coords + i] * sums[:, i * LANES : (i + 1) * LANES]
            solved.append(total)
        solved = jnp.concatenate(solved, axis=1).astype(BF16).astype(F32)
        return sums, solved

    def slot_message(solved):
        parts = [jnp.zeros((ROWS, LANES), F32) for _ in range(PACK // ROWS)]
        tails = []
        for s in range(slots):
            row = jnp.broadcast_to(solved[s : s + 1, :], (ROWS, points_wide)).astype(BF16)
            product = jnp.dot(row, jac_turned[s], preferred_element_type=F32)
            product = jnp.where(live[s], product, 0.0)
            for b in range(full):
                at, inside = divmod(b * slots + s, ROWS)
                parts[at] = jnp.where(
                    row8 == inside, product[:, b * LANES : (b + 1) * LANES], parts[at]
                )
            tails.append(product[:, full * LANES :])
        for i in range(slots // 2):
            at, inside = divmod(full * slots + i, ROWS)
            both = jnp.concatenate([tails[i], tails[i + slots // 2]], axis=1)
            parts[at] = jnp.where(row8 == inside, both, parts[at])
        return jnp.concatenate(parts, axis=0).astype(BF16)

    def energy_of(sums, solved):
        energy = sums * solved
        lanes = energy[:, :LANES]
        for i in range(1, coords):
            lanes = lanes + energy[:, i * LANES : (i + 1) * LANES]
        return jnp.sum(lanes * first_rows, axis=0, keepdims=True)

    live_wide = jnp.concatenate([live8] * (full + 1), axis=1)[:, :rows_wide]
    shared_wide = [
        jnp.concatenate([shared[s]] * (full + 1), axis=1)[:, :rows_wide] for s in range(slots)
    ]

    def send_slots(turn_no, message, reach):
        slot_send[turn_no] = message
        slot_recv[turn_no, 0] = message
        for delta, turn in peers:
            if abs(delta) <= reach:
                pltpu.make_async_remote_copy(
                    src_ref=slot_send.at[turn_no, pl.ds(0, slot_rows_sent)],
                    dst_ref=slot_recv.at[
                        turn_no, slot_index(-delta, -turn), pl.ds(0, slot_rows_sent)
                    ],
                    send_sem=slot_send_sem.at[turn_no],
                    recv_sem=slot_recv_sem.at[turn_no],
                    device_id=near(delta, turn),
                    device_id_type=MESH,
                ).start()

    def wait_slots(turn_no, count, sem):
        wait_bytes(
            slot_recv.at[turn_no, pl.ds(1, count - 1), pl.ds(0, slot_rows_sent)], sem.at[turn_no]
        )

    def received(turn_no, count):
        return slot_recv[turn_no, :count].reshape(count * PACK, LANES)

    def own_back(turn_no, count):
        width = count * PACK
        found = jnp.dot(
            choose_field[:, :width], received(turn_no, count), preferred_element_type=F32
        )
        tail_low = found[ROWS * tiles : ROWS * tiles + 16]
        tail_high = found[ROWS * tiles + 16 : ROWS * tiles + 32]
        lasts_low = tail_low + pltpu.roll(tail_high, CAM_TILE, 1)
        lasts_high = pltpu.roll(tail_low, CAM_TILE, 1) + tail_high
        parts = []
        for i in range(pairs):
            first = found[2 * ROWS * i : 2 * ROWS * i + ROWS]
            second = found[2 * ROWS * i + ROWS : 2 * ROWS * (i + 1)]
            top = jnp.where(
                low8,
                jnp.where(even8, first, pltpu.roll(first, CAM_TILE, 1)),
                jnp.where(even8, pltpu.roll(second, CAM_TILE, 1), second),
            )
            last = jnp.where(
                low1, lasts_low[2 * i : 2 * i + 1], lasts_high[2 * i + 1 : 2 * i + 2]
            )
            parts.append(jnp.concatenate([top, last], axis=0))
        return jnp.concatenate(parts, axis=1)

    field_bytes(0, field_recv_sem)
    wait_bytes(keys.at[first_keys], key_recv_sem.at[0])
    send_keys(second_wave, 1)
    _, solved = slot_rows(window_slots(0))
    send_slots(0, slot_message(solved), REACH)

    wait_bytes(keys.at[second_keys], key_recv_sem.at[1])
    lows, highs = [], []
    place_lane = lax.shift_right_logical(window_lane, 5)
    per_group = LANES // PACK
    order = [(delta, turn) for delta in ORDER for turn in range(grps)]
    for group in range(near_count // per_group):
        low = jnp.full((1, LANES), NONE, I32)
        high = jnp.full((1, LANES), NONE, I32)
        for j in range(per_group):
            delta, turn = order[group * per_group + j]
            key = keys[key_index[(delta, turn)]] + 8 * tiles * delta
            low = jnp.where(place_lane == j, key[0:1], low)
            high = jnp.where(place_lane == j, key[1:2], high)
        lows.append(low)
        highs.append(high)
    choose_slots[...] = matches(lows, highs)
    half_row = lax.shift_right_logical(row8, 1)
    heads = []
    for t in range(tiles):
        key = 8 * (tiles + t) + half_row
        heads.append(jnp.concatenate([(low == key).astype(F32) for low in lows], axis=1))
    tails = []
    for kind, found in ((full, lows), (full + 1, highs)):
        for at in (0, ROWS):
            key = jnp.where(row8 + at < tiles, 8 * (tiles + at + row8) + kind, -1)
            tails.append(jnp.concatenate([(lane == key).astype(F32) for lane in found], axis=1))
    choose_field[...] = jnp.concatenate(heads + tails, axis=0).astype(BF16)
    for f in (1, 2):
        field_bytes(f, field_recv_sem)
    start_slots = window_slots(1)
    scale_slots = window_slots(2)

    wait_slots(0, near_count, slot_recv_sem)
    back = slot_fields(choose_slots[...], received(0, near_count))
    own_found = own_back(0, near_count)
    direction_slots = start_slots + scale_slots * back
    _, solved = slot_rows(direction_slots)
    residual0 = residual0 + own_found
    direction = residual0 * scale
    product1 = block_product(direction)
    put_field(3, (product1 - diagonal * direction) * scale)
    for copy in field_copies(3):
        copy.start()
    field_bytes(1, field_send_sem)
    send_slots(1, slot_message(solved), REACH)
    field_bytes(3, field_recv_sem)
    change_slots = window_slots(3)

    wait_slots(1, near_count, slot_recv_sem)
    back = slot_fields(choose_slots[...], received(1, near_count))
    own_found = own_back(1, near_count)
    sums, solved = slot_rows(scale_slots * back - change_slots)
    send_slots(2, slot_message(solved), 1)
    field_bytes(2, field_send_sem)
    energy = energy_of(sums, solved)
    image1 = product1 - own_found
    trial = residual0 - image1
    shaped = trial * scale
    product2 = block_product(shaped)

    def lane_sum(field):
        total = field[:, :LANES]
        for i in range(1, pairs):
            total = total + field[:, i * LANES : (i + 1) * LANES]
        return jnp.sum(total, axis=0, keepdims=True) * (1.0 / grps)

    sums = jnp.zeros((ROWS, LANES), F32)
    for i, value in enumerate(
        (
            lane_sum(residual0 * direction),
            lane_sum(direction * image1),
            lane_sum(residual0 * shaped),
            lane_sum(trial * shaped),
            lane_sum(image1 * shaped),
            lane_sum(shaped * product2) - energy,
        )
    ):
        sums = jnp.where(row8 == i, value, sums)
    sums = jnp.sum(sums, axis=1, keepdims=True)
    own_sums = jnp.sum(jnp.where(row8 == lane8, sums, 0.0), axis=0, keepdims=True)
    scalar_send[...] = own_sums

    def send_scalars(index, device):
        pltpu.make_async_remote_copy(
            src_ref=scalar_send,
            dst_ref=scalar_recv.at[index],
            send_sem=scalar_sem.at[0],
            recv_sem=scalar_sem.at[1],
            device_id=device,
            device_id_type=MESH,
        ).start()

    everyone(send_scalars)

    wait_slots(2, close_count, slot_recv_sem)
    image2 = product2 - own_back(2, close_count)
    wait_bytes(scalar_recv, scalar_sem.at[1])
    totals = own_sums + jnp.sum(scalar_recv[...], axis=0)
    rz0, curve1, cross, trial_rz, mixed_sum, curve_w = [totals[:, i : i + 1] for i in range(6)]
    step1 = rz0 / curve1
    short = 1.0 - step1
    rz1 = short * short * rz0 + 2.0 * short * step1 * cross + step1 * step1 * trial_rz
    keep = short + rz1 / rz0
    curve2 = keep * keep * curve1 + 2.0 * keep * step1 * mixed_sum + step1 * step1 * curve_w
    step2 = rz1 / curve2
    near_part = step1 + step2 * keep
    far_part = step2 * step1
    solution_ref[...] = guess[...] + near_part * direction + far_part * shaped
    residual_ref[...] = residual0 - near_part * image1 - far_part * image2

    wait_bytes(scalar_recv, scalar_sem.at[0])
    for f in (0, 3):
        field_bytes(f, field_send_sem)
    wait_bytes(keys.at[first_keys], key_send_sem.at[0])
    wait_bytes(keys.at[second_keys], key_send_sem.at[1])
    for turn_no, count in enumerate((near_count, near_count, close_count)):
        wait_slots(turn_no, count, slot_send_sem)


def finish_kernel(first, second, solution_ref, residual_ref, sem):
    copies = [
        pltpu.make_async_copy(first, solution_ref, sem.at[0]),
        pltpu.make_async_copy(second, residual_ref, sem.at[1]),
    ]
    for copy in copies:
        copy.start()
    for copy in copies:
        copy.wait()


def finish(first, second):
    vmem = pl.BlockSpec(memory_space=pltpu.VMEM)
    hbm = pl.BlockSpec(memory_space=pltpu.HBM)
    shape = jax.ShapeDtypeStruct(first.shape, first.dtype)
    return pl.pallas_call(
        finish_kernel,
        out_shape=(shape, shape),
        in_specs=[vmem] * 2,
        out_specs=(hbm, hbm),
        scratch_shapes=[pltpu.SemaphoreType.DMA((2,))],
    )(*[pltpu.with_memory_space_constraint(x, pltpu.VMEM) for x in (first, second)])


def per_device(
    cells, grps, initial_guess, right_side, camera_blocks, point_inverse, jacobian_tiles, tile_pattern, cell_load
):
    params, cameras = initial_guess.shape
    slots, rows_wide, points_wide = jacobian_tiles.shape
    near = SPAN * grps
    tiles = cameras // CAM_TILE
    full = rows_wide // LANES
    field_pack = round_up(full * tiles + tiles // 2, 64)
    hbm = pl.BlockSpec(memory_space=pltpu.HBM)
    vmem = pl.BlockSpec(memory_space=pltpu.VMEM)
    dma = pltpu.SemaphoreType.DMA
    field = pltpu.VMEM((params, cameras), F32)
    first, second = pl.pallas_call(
        functools.partial(kernel, cells, grps),
        out_shape=(field, field),
        in_specs=[hbm] * 7,
        out_specs=(vmem, vmem),
        scratch_shapes=[
            pltpu.SMEM((2, slots), I32),
            pltpu.SMEM((1,), I32),
            pltpu.VMEM((params, cameras), F32),
            pltpu.VMEM((params, cameras), F32),
            pltpu.VMEM(camera_blocks.shape, F32),
            pltpu.VMEM(point_inverse.shape, F32),
            pltpu.VMEM(jacobian_tiles.shape, BF16),
            pltpu.VMEM((slots, points_wide, rows_wide), BF16),
            pltpu.VMEM((4, 3, field_pack, LANES), BF16),
            pltpu.VMEM((near, 2, LANES), I32),
            pltpu.VMEM((3, PACK, LANES), BF16),
            pltpu.VMEM((3, near, PACK, LANES), BF16),
            pltpu.VMEM((1, LANES), F32),
            pltpu.VMEM((cells * grps - 1, 1, LANES), F32),
            pltpu.VMEM((ROWS * (full + 2), near * PACK), BF16),
            pltpu.VMEM((ROWS * tiles + 32, near * PACK), BF16),
            pltpu.VMEM((ROWS * (full + 2), 3 * field_pack), BF16),
            dma((6,)),
            dma((slots,)),
            dma((4,)),
            dma((4,)),
            dma((2,)),
            dma((2,)),
            dma((3,)),
            dma((3,)),
            dma((2,)),
        ],
        compiler_params=pltpu.CompilerParams(collective_id=0, has_side_effects=True),
    )(initial_guess, right_side, camera_blocks, point_inverse, jacobian_tiles, tile_pattern.T, cell_load)
    return finish(first, second)


def solution(mesh):
    placed = (
        P(None, "cell"),
        P(None, "cell"),
        P(None, None, "cell"),
        P(None, None, ("cell", "grp")),
        P(("cell", "grp"), None, None),
        P(("cell", "grp"), None),
        P("cell"),
    )
    return jax.shard_map(
        functools.partial(per_device, mesh.shape["cell"], mesh.shape["grp"]),
        mesh=mesh,
        in_specs=placed,
        out_specs=(P(None, "cell"), P(None, "cell")),
        check_vma=False,
    )
```

```python
import functools

import jax
import jax.numpy as jnp
from jax import lax
from jax.experimental import pallas as pl
from jax.experimental.pallas import tpu as pltpu
from jax.sharding import PartitionSpec as P

CAM_TILE = 64
REACH = 2
SPAN = 2 * REACH + 1
ORDER = sorted(range(-REACH, REACH + 1), key=abs)
LANES = 128
ROWS = 8
PACK = 32
NONE = -(1 << 20)
MESH = pl.DeviceIdType.MESH
F32 = jnp.float32
BF16 = jnp.bfloat16
I32 = jnp.int32


def round_up(value, step):
    return (value + step - 1) // step * step


def kernel(
    cells,
    grps,
    guess_hbm,
    right_hbm,
    blocks_hbm,
    inverse_hbm,
    jac_hbm,
    pattern_hbm,
    load_hbm,
    solution_ref,
    residual_ref,
    pattern,
    load,
    guess,
    right,
    blocks,
    inverse,
    jac,
    jac_turned,
    jac_tails,
    fields,
    keys,
    slot_send,
    slot_recv,
    scalar_send,
    scalar_recv,
    choose_slots,
    choose_field,
    choose_window,
    local_sem,
    jac_sem,
    field_send_sem,
    field_recv_sem,
    key_send_sem,
    key_recv_sem,
    slot_send_sem,
    slot_recv_sem,
    scalar_sem,
):
    params, cameras = guess.shape
    slots, rows_wide, points_wide = jac.shape
    tiles = cameras // CAM_TILE
    pairs = cameras // LANES
    coords = inverse.shape[0]
    point_tiles = inverse.shape[2] // LANES
    full = rows_wide // LANES
    slot_rows_sent = round_up(full * slots + slots // 2, 4)
    field_rows = full * tiles + tiles // 2
    field_rows_sent = round_up(field_rows, ROWS)
    field_pack = fields.shape[2]
    near_count = SPAN * grps
    close_count = 3 * grps
    devices = cells * grps
    cell = lax.axis_index("cell")
    grp = lax.axis_index("grp")

    def near(delta, turn):
        return (lax.rem(cell + delta + cells, cells), lax.rem(grp + turn + grps, grps))

    def slot_index(delta, turn):
        return ORDER.index(delta) * grps + turn % grps

    peers = sorted(
        [(d, t) for d in ORDER for t in range(grps) if (d, t) != (0, 0)],
        key=lambda peer: ((abs(peer[0]) + REACH) % (REACH + 1), -peer[1]),
    )
    first_wave = [(d, t) for d, t in peers if d == 0 or t == 0]
    second_wave = [(d, t) for d, t in peers if d != 0 and t != 0]
    key_index = {(0, 0): 0}
    for delta, turn in first_wave + second_wave:
        key_index[(delta, turn)] = len(key_index)

    turned = [lax.rem(grp + turn, grps) for turn in range(grps)]

    def everyone(act):
        for turn in range(1, grps):
            act(turn - 1, (cell, turned[turn]))

        def one_cell(delta, carry):
            other = lax.rem(cell + delta, cells)
            for turn in range(grps):
                act(delta * grps + (turn - 1), (other, turned[turn]))
            return carry

        lax.fori_loop(1, cells, one_cell, 0)

    barrier = pltpu.get_barrier_semaphore()

    def greet(index, device):
        pl.semaphore_signal(barrier, inc=1, device_id=device, device_id_type=MESH)

    if cells // 2 <= 2 * REACH:
        greeted = len(first_wave)
        for delta, turn in first_wave:
            greet(0, near(delta, turn))
    else:
        greeted = devices - 1
        everyone(greet)

    local = [
        pltpu.make_async_copy(src, dst, local_sem.at[i])
        for i, (src, dst) in enumerate(
            (
                (guess_hbm, guess),
                (pattern_hbm, pattern),
                (load_hbm, load),
                (blocks_hbm, blocks),
                (right_hbm, right),
                (inverse_hbm, inverse),
            )
        )
    ]
    jac_copies = [
        pltpu.make_async_copy(jac_hbm.at[s], jac.at[s], jac_sem.at[s]) for s in range(slots)
    ]
    for copy in local:
        copy.start()
    for copy in jac_copies:
        copy.start()

    def iota(shape, axis):
        return lax.broadcasted_iota(I32, shape, axis)

    def steps(value, width, count):
        return sum((value >= width * j).astype(I32) for j in range(1, count + 1))

    lane8 = iota((ROWS, LANES), 1)
    row8 = iota((ROWS, LANES), 0)
    low8 = lane8 < CAM_TILE
    low1 = iota((1, LANES), 1) < CAM_TILE
    even8 = lax.bitwise_and(row8, 1) == 0

    fields[:, :, field_rows_sent:, :] = jnp.zeros(
        (fields.shape[0], 3, field_pack - field_rows_sent, LANES), BF16
    )
    slot_recv[:, :, slot_rows_sent:, :] = jnp.zeros(
        (3, near_count, PACK - slot_rows_sent, LANES), BF16
    )

    pick_row = iota((field_pack, LANES), 0)
    pick_chunk = steps(pick_row, tiles, full)
    pick_tile = pick_row - pick_chunk * tiles
    pick_tail = pick_chunk == full
    source_low = 16 * pick_tile + 2 * pick_chunk
    other_tile = jnp.where(pick_tail, pick_tile + tiles // 2, pick_tile)
    flipped = other_tile + 1 - 2 * lax.bitwise_and(other_tile, 1)
    source_high = 16 * flipped + jnp.where(pick_tail, 2 * full, 2 * pick_chunk + 1)
    unused = pick_row >= field_rows
    source_low = jnp.where(unused, -1, source_low)
    source_high = jnp.where(unused, -1, source_high)
    picked_width = 16 * tiles
    lane_pick = iota((field_pack, LANES), 1)

    def one_hot(source):
        parts = [
            (source == lane_pick + LANES * j).astype(F32)
            for j in range(round_up(picked_width, LANES) // LANES)
        ]
        return jnp.concatenate(parts, axis=1)[:, :picked_width].astype(BF16)

    spread = jnp.concatenate([one_hot(source_low), one_hot(source_high)], axis=0)

    def to_rows(field):
        tall = jnp.concatenate([field, jnp.zeros((16 - params, cameras), F32)], axis=0)
        parts = []
        for i in range(pairs):
            block = tall[:, i * LANES : (i + 1) * LANES]
            parts += [block.astype(BF16), pltpu.roll(block, CAM_TILE, 1).astype(BF16)]
        both = jnp.dot(spread, jnp.concatenate(parts, axis=0), preferred_element_type=F32)
        low = lane_pick < CAM_TILE
        picked = jnp.where(low, both[:field_pack], both[field_pack:])
        return picked[:field_rows_sent].astype(BF16)

    def put_field(f, field):
        fields[f, 2, :field_rows_sent] = to_rows(field)

    def field_copies(f):
        return [
            pltpu.make_async_remote_copy(
                src_ref=fields.at[f, 2, pl.ds(0, field_rows_sent)],
                dst_ref=fields.at[f, side, pl.ds(0, field_rows_sent)],
                send_sem=field_send_sem.at[f],
                recv_sem=field_recv_sem.at[f],
                device_id=near(delta, 0),
                device_id_type=MESH,
            )
            for side, delta in ((0, 1), (1, -1))
        ]

    def wait_bytes(ref, sem):
        pltpu.make_async_copy(ref, ref, sem).wait()

    def field_bytes(f, sem):
        wait_bytes(fields.at[f, pl.ds(0, 2), pl.ds(0, field_rows_sent)], sem.at[f])

    local[0].wait()
    put_field(0, guess[...])

    local[1].wait()
    local[2].wait()
    live = [s < load[0] for s in range(slots)]
    ids = [pattern[0, s] for s in range(slots)]
    point_ids = [pattern[1, s] for s in range(slots)]
    live_rows = jnp.zeros((ROWS, LANES), I32)
    id_rows = jnp.full((ROWS, LANES), NONE, I32)
    point_rows = jnp.full((ROWS, LANES), -1, I32)
    first_rows = jnp.zeros((ROWS, LANES), F32)
    for s in range(slots):
        here = row8 == s
        id_rows = jnp.where(here, jnp.where(live[s], 8 * ids[s], NONE), id_rows)
        point_rows = jnp.where(here, point_ids[s], point_rows)
        live_rows = jnp.where(here, jnp.where(live[s], 1, 0), live_rows)
        first = live[s]
        for u in range(s):
            same = jnp.logical_and(live[u], point_ids[u] == point_ids[s])
            first = jnp.logical_and(first, jnp.logical_not(same))
        first_rows = jnp.where(here, jnp.where(first, 1.0, 0.0), first_rows)
    live8 = live_rows > 0
    shared = [
        jnp.logical_and(point_rows == point_ids[s], jnp.where(live[s], 1, 0) > 0)
        for s in range(slots)
    ]

    key_lane = lax.bitwise_and(iota((2, LANES), 1), PACK - 1)
    key_chunk = steps(key_lane, slots, full)
    key_slot = key_lane - slots * key_chunk
    key_row = iota((2, LANES), 0)
    key_tail = jnp.logical_and(key_chunk == full, key_slot < slots // 2)
    own_key = jnp.full((2, LANES), NONE, I32)
    for s in range(slots):
        code = jnp.where(live[s], 8 * ids[s], NONE)
        head = jnp.logical_and(jnp.logical_and(key_chunk < full, key_slot == s), key_row == 0)
        tail_row, tail_slot = divmod(s, slots // 2)
        tail = jnp.logical_and(
            jnp.logical_and(key_tail, key_slot == tail_slot), key_row == tail_row
        )
        own_key = jnp.where(head, code + key_chunk, own_key)
        own_key = jnp.where(tail, code + full + tail_row, own_key)
    keys[0] = own_key

    row_keys = [id_rows + b for b in range(full + 2)]

    window_lane = iota((1, LANES), 1)
    window_parts = [[], []]
    window_width = 3 * field_pack
    for group in range(round_up(window_width, LANES) // LANES):
        position = window_lane + LANES * group
        place = steps(position, field_pack, 2)
        side = jnp.where(place == 0, 0, jnp.where(place == 1, 2, 1))
        row = position - place * field_pack
        chunk = steps(row, tiles, full)
        tile = side * tiles + row - chunk * tiles
        off = row >= field_rows
        tail = jnp.logical_and(chunk == full, jnp.logical_not(off))
        window_parts[0].append(jnp.where(off, -1, 8 * tile + chunk))
        window_parts[1].append(jnp.where(tail, 8 * (tile + tiles // 2) + full + 1, -1))
    window_low = window_parts[0]
    window_high = window_parts[1]

    def matches(low_keys, high_keys):
        parts = []
        for b in range(full + 2):
            found = low_keys if b <= full else high_keys
            parts.append(
                jnp.concatenate([(key == row_keys[b]).astype(F32) for key in found], axis=1)
            )
        return jnp.concatenate(parts, axis=0).astype(BF16)

    choose_window[...] = matches(window_low, window_high)[:, :window_width]

    def slot_fields(chosen, rows):
        found = jnp.dot(chosen, rows, preferred_element_type=F32)
        parts = [found[b * ROWS : (b + 1) * ROWS] for b in range(full + 2)]
        tail = parts[full] + pltpu.roll(parts[full + 1], CAM_TILE, 1)
        return jnp.concatenate(parts[:full] + [tail], axis=1)[:, :rows_wide]

    def window_slots(f):
        return slot_fields(choose_window[...], fields[f].reshape(window_width, LANES))

    def block_product(field):
        total = blocks[0] * field[0:1, :]
        for k in range(1, params):
            total = total + blocks[k] * field[k : k + 1, :]
        return total

    local[3].wait()
    row_wide = iota((params, cameras), 0)
    diagonal = blocks[0]
    for k in range(1, params):
        diagonal = jnp.where(row_wide == k, blocks[k], diagonal)
    scale = 1.0 / diagonal
    local[4].wait()
    residual0 = right[...] - block_product(guess[...])
    put_field(1, residual0 * scale)
    put_field(2, scale)
    local[5].wait()
    inverse_rows = []
    for j in range(coords):
        for i in range(coords):
            picked = jnp.zeros((ROWS, LANES), F32)
            for q in range(point_tiles):
                picked = jnp.where(
                    point_rows == q, inverse[j, i : i + 1, q * LANES : (q + 1) * LANES], picked
                )
            inverse_rows.append(picked)

    for copy in jac_copies:
        copy.wait()
    pl.semaphore_wait(barrier, greeted)

    for copy in field_copies(0):
        copy.start()

    def send_keys(wave, sem):
        for delta, turn in wave:
            pltpu.make_async_remote_copy(
                src_ref=keys.at[0],
                dst_ref=keys.at[key_index[(-delta, -turn % grps)]],
                send_sem=key_send_sem.at[sem],
                recv_sem=key_recv_sem.at[sem],
                device_id=near(delta, turn),
                device_id_type=MESH,
            ).start()

    first_keys = pl.ds(1, len(first_wave))
    second_keys = pl.ds(1 + len(first_wave), len(second_wave))
    send_keys(first_wave, 0)
    for f in (1, 2):
        for copy in field_copies(f):
            copy.start()
    wide = full * LANES
    for s in range(slots):
        jac_turned[s] = jac[s, :wide].T
    for i in range(slots // 2):
        both = jnp.concatenate([jac[i, wide:], jac[i + slots // 2, wide:]], axis=0)
        jac_tails[i] = both.T

    def slot_rows(values):
        values = jnp.where(live_wide, values, 0.0)
        sums = jnp.zeros((ROWS, points_wide), F32)
        rests = []
        for s in range(slots):
            spread_row = jnp.where(shared_wide[s], values[s : s + 1, :], 0.0)
            low_row = spread_row.astype(BF16)
            rests.append(low_row[:, full * LANES :])
            sums = sums + jnp.dot(
                low_row[:, : full * LANES], jac[s, : full * LANES], preferred_element_type=F32
            )
        rest = jnp.concatenate(rests, axis=1)
        sums = sums + jnp.dot(
            rest,
            jnp.concatenate([jac[s, full * LANES :] for s in range(slots)], axis=0),
            preferred_element_type=F32,
        )
        solved = []
        for j in range(coords):
            total = inverse_rows[j * coords] * sums[:, :LANES]
            for i in range(1, coords):
                total = total + inverse_rows[j * coords + i] * sums[:, i * LANES : (i + 1) * LANES]
            solved.append(total)
        solved = jnp.concatenate(solved, axis=1).astype(BF16).astype(F32)
        return sums, solved

    def slot_message(solved):
        parts = [jnp.zeros((ROWS, LANES), F32) for _ in range(PACK // ROWS)]
        for s in range(slots):
            row = jnp.broadcast_to(solved[s : s + 1, :], (ROWS, points_wide)).astype(BF16)
            product = jnp.dot(row, jac_turned[s], preferred_element_type=F32)
            product = jnp.where(live[s], product, 0.0)
            for b in range(full):
                at, inside = divmod(b * slots + s, ROWS)
                parts[at] = jnp.where(
                    row8 == inside, product[:, b * LANES : (b + 1) * LANES], parts[at]
                )
        short = solved.astype(BF16)
        for i in range(slots // 2):
            at, inside = divmod(full * slots + i, ROWS)
            product = jnp.dot(short, jac_tails[i], preferred_element_type=F32)
            product = jnp.where(live8, product, 0.0)
            other = i + slots // 2
            both = jnp.where(low1, product[i : i + 1], product[other : other + 1])
            parts[at] = jnp.where(row8 == inside, both, parts[at])
        return jnp.concatenate(parts, axis=0).astype(BF16)

    def energy_of(sums, solved):
        energy = sums * solved
        lanes = energy[:, :LANES]
        for i in range(1, coords):
            lanes = lanes + energy[:, i * LANES : (i + 1) * LANES]
        return jnp.sum(lanes * first_rows, axis=0, keepdims=True)

    live_wide = jnp.concatenate([live8] * (full + 1), axis=1)[:, :rows_wide]
    shared_wide = [
        jnp.concatenate([shared[s]] * (full + 1), axis=1)[:, :rows_wide] for s in range(slots)
    ]

    def send_slots(turn_no, message, reach):
        slot_send[turn_no] = message
        slot_recv[turn_no, 0] = message
        for delta, turn in peers:
            if abs(delta) <= reach:
                pltpu.make_async_remote_copy(
                    src_ref=slot_send.at[turn_no, pl.ds(0, slot_rows_sent)],
                    dst_ref=slot_recv.at[
                        turn_no, slot_index(-delta, -turn), pl.ds(0, slot_rows_sent)
                    ],
                    send_sem=slot_send_sem.at[turn_no],
                    recv_sem=slot_recv_sem.at[turn_no],
                    device_id=near(delta, turn),
                    device_id_type=MESH,
                ).start()

    def wait_slots(turn_no, count, sem):
        wait_bytes(
            slot_recv.at[turn_no, pl.ds(1, count - 1), pl.ds(0, slot_rows_sent)], sem.at[turn_no]
        )

    def received(turn_no, count):
        return slot_recv[turn_no, :count].reshape(count * PACK, LANES)

    def own_back(turn_no, count):
        width = count * PACK
        found = jnp.dot(
            choose_field[:, :width], received(turn_no, count), preferred_element_type=F32
        )
        tail_low = found[ROWS * tiles : ROWS * tiles + 16]
        tail_high = found[ROWS * tiles + 16 : ROWS * tiles + 32]
        lasts_low = tail_low + pltpu.roll(tail_high, CAM_TILE, 1)
        lasts_high = pltpu.roll(tail_low, CAM_TILE, 1) + tail_high
        parts = []
        for i in range(pairs):
            first = found[2 * ROWS * i : 2 * ROWS * i + ROWS]
            second = found[2 * ROWS * i + ROWS : 2 * ROWS * (i + 1)]
            top = jnp.where(
                low8,
                jnp.where(even8, first, pltpu.roll(first, CAM_TILE, 1)),
                jnp.where(even8, pltpu.roll(second, CAM_TILE, 1), second),
            )
            last = jnp.where(
                low1, lasts_low[2 * i : 2 * i + 1], lasts_high[2 * i + 1 : 2 * i + 2]
            )
            parts.append(jnp.concatenate([top, last], axis=0))
        return jnp.concatenate(parts, axis=1)

    field_bytes(0, field_recv_sem)
    wait_bytes(keys.at[first_keys], key_recv_sem.at[0])
    send_keys(second_wave, 1)
    _, solved = slot_rows(window_slots(0))
    send_slots(0, slot_message(solved), REACH)

    wait_bytes(keys.at[second_keys], key_recv_sem.at[1])
    lows, highs = [], []
    place_lane = lax.shift_right_logical(window_lane, 5)
    per_group = LANES // PACK
    order = [(delta, turn) for delta in ORDER for turn in range(grps)]
    for group in range(near_count // per_group):
        low = jnp.full((1, LANES), NONE, I32)
        high = jnp.full((1, LANES), NONE, I32)
        for j in range(per_group):
            delta, turn = order[group * per_group + j]
            key = keys[key_index[(delta, turn)]] + 8 * tiles * delta
            low = jnp.where(place_lane == j, key[0:1], low)
            high = jnp.where(place_lane == j, key[1:2], high)
        lows.append(low)
        highs.append(high)
    choose_slots[...] = matches(lows, highs)
    half_row = lax.shift_right_logical(row8, 1)
    heads = []
    for t in range(tiles):
        key = 8 * (tiles + t) + half_row
        heads.append(jnp.concatenate([(low == key).astype(F32) for low in lows], axis=1))
    tails = []
    for kind, found in ((full, lows), (full + 1, highs)):
        for at in (0, ROWS):
            key = jnp.where(row8 + at < tiles, 8 * (tiles + at + row8) + kind, -1)
            tails.append(jnp.concatenate([(lane == key).astype(F32) for lane in found], axis=1))
    choose_field[...] = jnp.concatenate(heads + tails, axis=0).astype(BF16)
    for f in (1, 2):
        field_bytes(f, field_recv_sem)
    start_slots = window_slots(1)
    scale_slots = window_slots(2)

    wait_slots(0, near_count, slot_recv_sem)
    back = slot_fields(choose_slots[...], received(0, near_count))
    own_found = own_back(0, near_count)
    direction_slots = start_slots + scale_slots * back
    _, solved = slot_rows(direction_slots)
    residual0 = residual0 + own_found
    direction = residual0 * scale
    product1 = block_product(direction)
    put_field(3, (product1 - diagonal * direction) * scale)
    for copy in field_copies(3):
        copy.start()
    field_bytes(1, field_send_sem)
    send_slots(1, slot_message(solved), REACH)
    field_bytes(3, field_recv_sem)
    change_slots = window_slots(3)

    wait_slots(1, near_count, slot_recv_sem)
    back = slot_fields(choose_slots[...], received(1, near_count))
    own_found = own_back(1, near_count)
    sums, solved = slot_rows(scale_slots * back - change_slots)
    send_slots(2, slot_message(solved), 1)
    field_bytes(2, field_send_sem)
    energy = energy_of(sums, solved)
    image1 = product1 - own_found
    trial = residual0 - image1
    shaped = trial * scale
    product2 = block_product(shaped)

    def lane_sum(field):
        total = field[:, :LANES]
        for i in range(1, pairs):
            total = total + field[:, i * LANES : (i + 1) * LANES]
        return jnp.sum(total, axis=0, keepdims=True) * (1.0 / grps)

    sums = jnp.zeros((ROWS, LANES), F32)
    for i, value in enumerate(
        (
            lane_sum(residual0 * direction),
            lane_sum(direction * image1),
            lane_sum(residual0 * shaped),
            lane_sum(trial * shaped),
            lane_sum(image1 * shaped),
            lane_sum(shaped * product2) - energy,
        )
    ):
        sums = jnp.where(row8 == i, value, sums)
    sums = jnp.sum(sums, axis=1, keepdims=True)
    own_sums = jnp.sum(jnp.where(row8 == lane8, sums, 0.0), axis=0, keepdims=True)
    scalar_send[...] = own_sums

    def send_scalars(index, device):
        pltpu.make_async_remote_copy(
            src_ref=scalar_send,
            dst_ref=scalar_recv.at[index],
            send_sem=scalar_sem.at[0],
            recv_sem=scalar_sem.at[1],
            device_id=device,
            device_id_type=MESH,
        ).start()

    everyone(send_scalars)

    wait_slots(2, close_count, slot_recv_sem)
    image2 = product2 - own_back(2, close_count)
    wait_bytes(scalar_recv, scalar_sem.at[1])
    totals = own_sums + jnp.sum(scalar_recv[...], axis=0)
    rz0, curve1, cross, trial_rz, mixed_sum, curve_w = [totals[:, i : i + 1] for i in range(6)]
    step1 = rz0 / curve1
    short = 1.0 - step1
    rz1 = short * short * rz0 + 2.0 * short * step1 * cross + step1 * step1 * trial_rz
    keep = short + rz1 / rz0
    curve2 = keep * keep * curve1 + 2.0 * keep * step1 * mixed_sum + step1 * step1 * curve_w
    step2 = rz1 / curve2
    near_part = step1 + step2 * keep
    far_part = step2 * step1
    solution_ref[...] = guess[...] + near_part * direction + far_part * shaped
    residual_ref[...] = residual0 - near_part * image1 - far_part * image2

    wait_bytes(scalar_recv, scalar_sem.at[0])
    for f in (0, 3):
        field_bytes(f, field_send_sem)
    wait_bytes(keys.at[first_keys], key_send_sem.at[0])
    wait_bytes(keys.at[second_keys], key_send_sem.at[1])
    for turn_no, count in enumerate((near_count, near_count, close_count)):
        wait_slots(turn_no, count, slot_send_sem)


def finish_kernel(first, second, solution_ref, residual_ref, sem):
    copies = [
        pltpu.make_async_copy(first, solution_ref, sem.at[0]),
        pltpu.make_async_copy(second, residual_ref, sem.at[1]),
    ]
    for copy in copies:
        copy.start()
    for copy in copies:
        copy.wait()


def finish(first, second):
    vmem = pl.BlockSpec(memory_space=pltpu.VMEM)
    hbm = pl.BlockSpec(memory_space=pltpu.HBM)
    shape = jax.ShapeDtypeStruct(first.shape, first.dtype)
    return pl.pallas_call(
        finish_kernel,
        out_shape=(shape, shape),
        in_specs=[vmem] * 2,
        out_specs=(hbm, hbm),
        scratch_shapes=[pltpu.SemaphoreType.DMA((2,))],
    )(*[pltpu.with_memory_space_constraint(x, pltpu.VMEM) for x in (first, second)])


def per_device(
    cells, grps, initial_guess, right_side, camera_blocks, point_inverse, jacobian_tiles, tile_pattern, cell_load
):
    params, cameras = initial_guess.shape
    slots, rows_wide, points_wide = jacobian_tiles.shape
    near = SPAN * grps
    tiles = cameras // CAM_TILE
    full = rows_wide // LANES
    field_pack = round_up(full * tiles + tiles // 2, 64)
    hbm = pl.BlockSpec(memory_space=pltpu.HBM)
    vmem = pl.BlockSpec(memory_space=pltpu.VMEM)
    dma = pltpu.SemaphoreType.DMA
    field = pltpu.VMEM((params, cameras), F32)
    first, second = pl.pallas_call(
        functools.partial(kernel, cells, grps),
        out_shape=(field, field),
        in_specs=[hbm] * 7,
        out_specs=(vmem, vmem),
        scratch_shapes=[
            pltpu.SMEM((2, slots), I32),
            pltpu.SMEM((1,), I32),
            pltpu.VMEM((params, cameras), F32),
            pltpu.VMEM((params, cameras), F32),
            pltpu.VMEM(camera_blocks.shape, F32),
            pltpu.VMEM(point_inverse.shape, F32),
            pltpu.VMEM(jacobian_tiles.shape, BF16),
            pltpu.VMEM((slots, points_wide, full * LANES), BF16),
            pltpu.VMEM((slots // 2, points_wide, LANES), BF16),
            pltpu.VMEM((4, 3, field_pack, LANES), BF16),
            pltpu.VMEM((near, 2, LANES), I32),
            pltpu.VMEM((3, PACK, LANES), BF16),
            pltpu.VMEM((3, near, PACK, LANES), BF16),
            pltpu.VMEM((1, LANES), F32),
            pltpu.VMEM((cells * grps - 1, 1, LANES), F32),
            pltpu.VMEM((ROWS * (full + 2), near * PACK), BF16),
            pltpu.VMEM((ROWS * tiles + 32, near * PACK), BF16),
            pltpu.VMEM((ROWS * (full + 2), 3 * field_pack), BF16),
            dma((6,)),
            dma((slots,)),
            dma((4,)),
            dma((4,)),
            dma((2,)),
            dma((2,)),
            dma((3,)),
            dma((3,)),
            dma((2,)),
        ],
        compiler_params=pltpu.CompilerParams(collective_id=0, has_side_effects=True),
    )(initial_guess, right_side, camera_blocks, point_inverse, jacobian_tiles, tile_pattern.T, cell_load)
    return finish(first, second)


def solution(mesh):
    placed = (
        P(None, "cell"),
        P(None, "cell"),
        P(None, None, "cell"),
        P(None, None, ("cell", "grp")),
        P(("cell", "grp"), None, None),
        P(("cell", "grp"), None),
        P("cell"),
    )
    return jax.shard_map(
        functools.partial(per_device, mesh.shape["cell"], mesh.shape["grp"]),
        mesh=mesh,
        in_specs=placed,
        out_specs=(P(None, "cell"), P(None, "cell")),
        check_vma=False,
    )
```

```python
import functools

import jax
import jax.numpy as jnp
from jax import lax
from jax.experimental import pallas as pl
from jax.experimental.pallas import tpu as pltpu
from jax.sharding import PartitionSpec as P

CAM_TILE = 64
REACH = 2
SPAN = 2 * REACH + 1
ORDER = sorted(range(-REACH, REACH + 1), key=abs)
LANES = 128
ROWS = 8
PACK = 32
NONE = -(1 << 20)
MESH = pl.DeviceIdType.MESH
F32 = jnp.float32
BF16 = jnp.bfloat16
I32 = jnp.int32


def round_up(value, step):
    return (value + step - 1) // step * step


def kernel(
    cells,
    grps,
    guess_hbm,
    right_hbm,
    blocks_hbm,
    inverse_hbm,
    jac_hbm,
    pattern_hbm,
    load_hbm,
    solution_ref,
    residual_ref,
    pattern,
    load,
    guess,
    right,
    blocks,
    inverse,
    jac,
    jac_turned,
    jac_tails,
    fields,
    keys,
    slot_send,
    slot_recv,
    scalar_send,
    scalar_recv,
    choose_slots,
    choose_field,
    choose_window,
    local_sem,
    jac_sem,
    field_send_sem,
    field_recv_sem,
    key_send_sem,
    key_recv_sem,
    slot_send_sem,
    slot_recv_sem,
    scalar_sem,
):
    params, cameras = guess.shape
    slots, rows_wide, points_wide = jac.shape
    tiles = cameras // CAM_TILE
    pairs = cameras // LANES
    coords = inverse.shape[0]
    point_tiles = inverse.shape[2] // LANES
    full = rows_wide // LANES
    slot_rows_sent = round_up(full * slots + slots // 2, 4)
    field_rows = full * tiles + tiles // 2
    field_rows_sent = round_up(field_rows, ROWS)
    field_pack = fields.shape[2]
    near_count = SPAN * grps
    close_count = 3 * grps
    devices = cells * grps
    cell = lax.axis_index("cell")
    grp = lax.axis_index("grp")

    def near(delta, turn):
        return (lax.rem(cell + delta + cells, cells), lax.rem(grp + turn + grps, grps))

    def slot_index(delta, turn):
        return ORDER.index(delta) * grps + turn % grps

    peers = sorted(
        [(d, t) for d in ORDER for t in range(grps) if (d, t) != (0, 0)],
        key=lambda peer: ((abs(peer[0]) + REACH) % (REACH + 1), -peer[1]),
    )
    first_wave = [(d, t) for d, t in peers if d == 0 or t == 0]
    second_wave = [(d, t) for d, t in peers if d != 0 and t != 0]
    key_index = {(0, 0): 0}
    for delta, turn in first_wave + second_wave:
        key_index[(delta, turn)] = len(key_index)

    turned = [lax.rem(grp + turn, grps) for turn in range(grps)]

    def everyone(act):
        for turn in range(1, grps):
            act(turn - 1, (cell, turned[turn]))

        def one_cell(delta, carry):
            other = lax.rem(cell + delta, cells)
            for turn in range(grps):
                act(delta * grps + (turn - 1), (other, turned[turn]))
            return carry

        lax.fori_loop(1, cells, one_cell, 0)

    barrier = pltpu.get_barrier_semaphore()

    def greet(index, device):
        pl.semaphore_signal(barrier, inc=1, device_id=device, device_id_type=MESH)

    if cells // 2 <= 2 * REACH:
        greeted = len(first_wave)
        for delta, turn in first_wave:
            greet(0, near(delta, turn))
    else:
        greeted = devices - 1
        everyone(greet)

    local = [
        pltpu.make_async_copy(src, dst, local_sem.at[i])
        for i, (src, dst) in enumerate(
            (
                (guess_hbm, guess),
                (pattern_hbm, pattern),
                (load_hbm, load),
                (blocks_hbm, blocks),
                (right_hbm, right),
                (inverse_hbm, inverse),
            )
        )
    ]
    jac_copies = [
        pltpu.make_async_copy(jac_hbm.at[s], jac.at[s], jac_sem.at[s]) for s in range(slots)
    ]
    for copy in local:
        copy.start()
    for copy in jac_copies:
        copy.start()

    def iota(shape, axis):
        return lax.broadcasted_iota(I32, shape, axis)

    def steps(value, width, count):
        return sum((value >= width * j).astype(I32) for j in range(1, count + 1))

    lane8 = iota((ROWS, LANES), 1)
    row8 = iota((ROWS, LANES), 0)
    low8 = lane8 < CAM_TILE
    low1 = iota((1, LANES), 1) < CAM_TILE
    even8 = lax.bitwise_and(row8, 1) == 0

    fields[:, :, field_rows_sent:, :] = jnp.zeros(
        (fields.shape[0], 3, field_pack - field_rows_sent, LANES), BF16
    )
    slot_recv[:, :, slot_rows_sent:, :] = jnp.zeros(
        (3, near_count, PACK - slot_rows_sent, LANES), BF16
    )

    pick_row = iota((field_pack, LANES), 0)
    pick_chunk = steps(pick_row, tiles, full)
    pick_tile = pick_row - pick_chunk * tiles
    pick_tail = pick_chunk == full
    source_low = 16 * pick_tile + 2 * pick_chunk
    other_tile = jnp.where(pick_tail, pick_tile + tiles // 2, pick_tile)
    flipped = other_tile + 1 - 2 * lax.bitwise_and(other_tile, 1)
    source_high = 16 * flipped + jnp.where(pick_tail, 2 * full, 2 * pick_chunk + 1)
    unused = pick_row >= field_rows
    source_low = jnp.where(unused, -1, source_low)
    source_high = jnp.where(unused, -1, source_high)
    picked_width = 16 * tiles
    lane_pick = iota((field_pack, LANES), 1)

    def one_hot(source):
        parts = [
            (source == lane_pick + LANES * j).astype(F32)
            for j in range(round_up(picked_width, LANES) // LANES)
        ]
        return jnp.concatenate(parts, axis=1)[:, :picked_width].astype(BF16)

    spread = jnp.concatenate([one_hot(source_low), one_hot(source_high)], axis=0)

    def to_rows(field):
        tall = jnp.concatenate([field, jnp.zeros((16 - params, cameras), F32)], axis=0)
        parts = []
        for i in range(pairs):
            block = tall[:, i * LANES : (i + 1) * LANES]
            parts += [block.astype(BF16), pltpu.roll(block, CAM_TILE, 1).astype(BF16)]
        both = jnp.dot(spread, jnp.concatenate(parts, axis=0), preferred_element_type=F32)
        low = lane_pick < CAM_TILE
        picked = jnp.where(low, both[:field_pack], both[field_pack:])
        return picked[:field_rows_sent].astype(BF16)

    def put_field(f, field):
        fields[f, 2, :field_rows_sent] = to_rows(field)

    def field_copies(f):
        return [
            pltpu.make_async_remote_copy(
                src_ref=fields.at[f, 2, pl.ds(0, field_rows_sent)],
                dst_ref=fields.at[f, side, pl.ds(0, field_rows_sent)],
                send_sem=field_send_sem.at[f],
                recv_sem=field_recv_sem.at[f],
                device_id=near(delta, 0),
                device_id_type=MESH,
            )
            for side, delta in ((0, 1), (1, -1))
        ]

    def wait_bytes(ref, sem):
        pltpu.make_async_copy(ref, ref, sem).wait()

    def field_bytes(f, sem):
        wait_bytes(fields.at[f, pl.ds(0, 2), pl.ds(0, field_rows_sent)], sem.at[f])

    local[0].wait()
    put_field(0, guess[...])

    local[1].wait()
    local[2].wait()
    live = [s < load[0] for s in range(slots)]
    ids = [pattern[0, s] for s in range(slots)]
    point_ids = [pattern[1, s] for s in range(slots)]
    live_rows = jnp.zeros((ROWS, LANES), I32)
    id_rows = jnp.full((ROWS, LANES), NONE, I32)
    point_rows = jnp.full((ROWS, LANES), -1, I32)
    first_rows = jnp.zeros((ROWS, LANES), F32)
    for s in range(slots):
        here = row8 == s
        id_rows = jnp.where(here, jnp.where(live[s], 8 * ids[s], NONE), id_rows)
        point_rows = jnp.where(here, point_ids[s], point_rows)
        live_rows = jnp.where(here, jnp.where(live[s], 1, 0), live_rows)
        first = live[s]
        for u in range(s):
            same = jnp.logical_and(live[u], point_ids[u] == point_ids[s])
            first = jnp.logical_and(first, jnp.logical_not(same))
        first_rows = jnp.where(here, jnp.where(first, 1.0, 0.0), first_rows)
    live8 = live_rows > 0
    shared = [
        jnp.logical_and(point_rows == point_ids[s], jnp.where(live[s], 1, 0) > 0)
        for s in range(slots)
    ]

    key_lane = lax.bitwise_and(iota((2, LANES), 1), PACK - 1)
    key_chunk = steps(key_lane, slots, full)
    key_slot = key_lane - slots * key_chunk
    key_row = iota((2, LANES), 0)
    key_tail = jnp.logical_and(key_chunk == full, key_slot < slots // 2)
    own_key = jnp.full((2, LANES), NONE, I32)
    for s in range(slots):
        code = jnp.where(live[s], 8 * ids[s], NONE)
        head = jnp.logical_and(jnp.logical_and(key_chunk < full, key_slot == s), key_row == 0)
        tail_row, tail_slot = divmod(s, slots // 2)
        tail = jnp.logical_and(
            jnp.logical_and(key_tail, key_slot == tail_slot), key_row == tail_row
        )
        own_key = jnp.where(head, code + key_chunk, own_key)
        own_key = jnp.where(tail, code + full + tail_row, own_key)
    keys[0] = own_key

    row_keys = [id_rows + b for b in range(full + 2)]

    window_lane = iota((1, LANES), 1)
    window_parts = [[], []]
    window_width = 3 * field_pack
    for group in range(round_up(window_width, LANES) // LANES):
        position = window_lane + LANES * group
        place = steps(position, field_pack, 2)
        side = jnp.where(place == 0, 0, jnp.where(place == 1, 2, 1))
        row = position - place * field_pack
        chunk = steps(row, tiles, full)
        tile = side * tiles + row - chunk * tiles
        off = row >= field_rows
        tail = jnp.logical_and(chunk == full, jnp.logical_not(off))
        window_parts[0].append(jnp.where(off, -1, 8 * tile + chunk))
        window_parts[1].append(jnp.where(tail, 8 * (tile + tiles // 2) + full + 1, -1))
    window_low = window_parts[0]
    window_high = window_parts[1]

    def matches(low_keys, high_keys):
        parts = []
        for b in range(full + 2):
            found = low_keys if b <= full else high_keys
            parts.append(
                jnp.concatenate([(key == row_keys[b]).astype(F32) for key in found], axis=1)
            )
        return jnp.concatenate(parts, axis=0).astype(BF16)

    choose_window[...] = matches(window_low, window_high)[:, :window_width]

    def slot_fields(chosen, rows):
        found = jnp.dot(chosen, rows, preferred_element_type=F32)
        parts = [found[b * ROWS : (b + 1) * ROWS] for b in range(full + 2)]
        tail = parts[full] + pltpu.roll(parts[full + 1], CAM_TILE, 1)
        return jnp.concatenate(parts[:full] + [tail], axis=1)[:, :rows_wide]

    def window_slots(f):
        return slot_fields(choose_window[...], fields[f].reshape(window_width, LANES))

    def block_product(field):
        total = blocks[0] * field[0:1, :]
        for k in range(1, params):
            total = total + blocks[k] * field[k : k + 1, :]
        return total

    local[3].wait()
    row_wide = iota((params, cameras), 0)
    diagonal = blocks[0]
    for k in range(1, params):
        diagonal = jnp.where(row_wide == k, blocks[k], diagonal)
    scale = 1.0 / diagonal
    local[4].wait()
    residual0 = right[...] - block_product(guess[...])
    put_field(1, residual0 * scale)
    put_field(2, scale)
    local[5].wait()
    inverse_rows = []
    for j in range(coords):
        for i in range(coords):
            picked = jnp.zeros((ROWS, LANES), F32)
            for q in range(point_tiles):
                picked = jnp.where(
                    point_rows == q, inverse[j, i : i + 1, q * LANES : (q + 1) * LANES], picked
                )
            inverse_rows.append(picked)

    for copy in jac_copies:
        copy.wait()
    pl.semaphore_wait(barrier, greeted)

    for copy in field_copies(0):
        copy.start()

    def send_keys(wave, sem):
        for delta, turn in wave:
            pltpu.make_async_remote_copy(
                src_ref=keys.at[0],
                dst_ref=keys.at[key_index[(-delta, -turn % grps)]],
                send_sem=key_send_sem.at[sem],
                recv_sem=key_recv_sem.at[sem],
                device_id=near(delta, turn),
                device_id_type=MESH,
            ).start()

    first_keys = pl.ds(1, len(first_wave))
    second_keys = pl.ds(1 + len(first_wave), len(second_wave))
    send_keys(first_wave, 0)
    for f in (1, 2):
        for copy in field_copies(f):
            copy.start()
    wide = full * LANES
    for s in range(slots):
        jac_turned[s] = jac[s, :wide].T
    spare = jac_tails.shape[1] - slots // 2 * LANES
    if spare:
        jac_tails[:, slots // 2 * LANES :] = jnp.zeros((points_wide, spare), BF16)
    for i in range(slots // 2):
        both = jnp.concatenate([jac[i, wide:], jac[i + slots // 2, wide:]], axis=0)
        jac_tails[:, i * LANES : (i + 1) * LANES] = both.T

    def slot_rows(values):
        values = jnp.where(live_wide, values, 0.0)
        half = slots // 2
        wide = full * LANES
        split = points_wide // (2 * LANES) * (2 * LANES)
        rows = [jnp.where(shared_wide[s], values[s : s + 1, :], 0.0) for s in range(slots)]
        left = jnp.zeros((ROWS, split), F32)
        right = jnp.zeros((ROWS, points_wide - split), F32)
        for i in range(half):
            u = i + half
            both = jnp.concatenate([rows[i][:, :wide], rows[u][:, :wide]], axis=0).astype(BF16)
            found = jnp.dot(
                both,
                jnp.concatenate([jac[i, :wide], jac[u, :wide]], axis=1),
                preferred_element_type=F32,
            )
            total = found[:ROWS, :points_wide] + found[ROWS:, points_wide:]
            left = left + total[:, :split]
            right = right + total[:, split:]
        rest = jnp.concatenate([row[:, wide:].astype(BF16) for row in rows], axis=1)
        sums = jnp.concatenate([left, right], axis=1) + jnp.dot(
            rest,
            jnp.concatenate([jac[s, wide:] for s in range(slots)], axis=0),
            preferred_element_type=F32,
        )
        solved = []
        for j in range(coords):
            total = inverse_rows[j * coords] * sums[:, :LANES]
            for i in range(1, coords):
                total = total + inverse_rows[j * coords + i] * sums[:, i * LANES : (i + 1) * LANES]
            solved.append(total)
        solved = jnp.concatenate(solved, axis=1).astype(BF16).astype(F32)
        return sums, solved

    def slot_message(solved):
        parts = [jnp.zeros((ROWS, LANES), F32) for _ in range(PACK // ROWS)]
        for s in range(slots):
            row = jnp.broadcast_to(solved[s : s + 1, :], (ROWS, points_wide)).astype(BF16)
            product = jnp.dot(row, jac_turned[s], preferred_element_type=F32)
            product = jnp.where(live[s], product, 0.0)
            for b in range(full):
                at, inside = divmod(b * slots + s, ROWS)
                parts[at] = jnp.where(
                    row8 == inside, product[:, b * LANES : (b + 1) * LANES], parts[at]
                )
        shorts = jnp.dot(solved.astype(BF16), jac_tails[...], preferred_element_type=F32)
        for i in range(slots // 2):
            at, inside = divmod(full * slots + i, ROWS)
            product = jnp.where(live8, shorts[:, i * LANES : (i + 1) * LANES], 0.0)
            other = i + slots // 2
            both = jnp.where(low1, product[i : i + 1], product[other : other + 1])
            parts[at] = jnp.where(row8 == inside, both, parts[at])
        return jnp.concatenate(parts, axis=0).astype(BF16)

    def energy_of(sums, solved):
        energy = sums * solved
        lanes = energy[:, :LANES]
        for i in range(1, coords):
            lanes = lanes + energy[:, i * LANES : (i + 1) * LANES]
        return jnp.sum(lanes * first_rows, axis=0, keepdims=True)

    live_wide = jnp.concatenate([live8] * (full + 1), axis=1)[:, :rows_wide]
    shared_wide = [
        jnp.concatenate([shared[s]] * (full + 1), axis=1)[:, :rows_wide] for s in range(slots)
    ]

    def send_slots(turn_no, message, reach):
        slot_send[turn_no] = message
        slot_recv[turn_no, 0] = message
        for delta, turn in peers:
            if abs(delta) <= reach:
                pltpu.make_async_remote_copy(
                    src_ref=slot_send.at[turn_no, pl.ds(0, slot_rows_sent)],
                    dst_ref=slot_recv.at[
                        turn_no, slot_index(-delta, -turn), pl.ds(0, slot_rows_sent)
                    ],
                    send_sem=slot_send_sem.at[turn_no],
                    recv_sem=slot_recv_sem.at[turn_no],
                    device_id=near(delta, turn),
                    device_id_type=MESH,
                ).start()

    def wait_slots(turn_no, count, sem):
        wait_bytes(
            slot_recv.at[turn_no, pl.ds(1, count - 1), pl.ds(0, slot_rows_sent)], sem.at[turn_no]
        )

    def received(turn_no, count):
        return slot_recv[turn_no, :count].reshape(count * PACK, LANES)

    def own_back(turn_no, count):
        width = count * PACK
        found = jnp.dot(
            choose_field[:, :width], received(turn_no, count), preferred_element_type=F32
        )
        tail_low = found[ROWS * tiles : ROWS * tiles + 16]
        tail_high = found[ROWS * tiles + 16 : ROWS * tiles + 32]
        lasts_low = tail_low + pltpu.roll(tail_high, CAM_TILE, 1)
        lasts_high = pltpu.roll(tail_low, CAM_TILE, 1) + tail_high
        parts = []
        for i in range(pairs):
            first = found[2 * ROWS * i : 2 * ROWS * i + ROWS]
            second = found[2 * ROWS * i + ROWS : 2 * ROWS * (i + 1)]
            top = jnp.where(
                low8,
                jnp.where(even8, first, pltpu.roll(first, CAM_TILE, 1)),
                jnp.where(even8, pltpu.roll(second, CAM_TILE, 1), second),
            )
            last = jnp.where(
                low1, lasts_low[2 * i : 2 * i + 1], lasts_high[2 * i + 1 : 2 * i + 2]
            )
            parts.append(jnp.concatenate([top, last], axis=0))
        return jnp.concatenate(parts, axis=1)

    field_bytes(0, field_recv_sem)
    wait_bytes(keys.at[first_keys], key_recv_sem.at[0])
    send_keys(second_wave, 1)
    _, solved = slot_rows(window_slots(0))
    send_slots(0, slot_message(solved), REACH)

    wait_bytes(keys.at[second_keys], key_recv_sem.at[1])
    lows, highs = [], []
    place_lane = lax.shift_right_logical(window_lane, 5)
    per_group = LANES // PACK
    order = [(delta, turn) for delta in ORDER for turn in range(grps)]
    for group in range(near_count // per_group):
        low = jnp.full((1, LANES), NONE, I32)
        high = jnp.full((1, LANES), NONE, I32)
        for j in range(per_group):
            delta, turn = order[group * per_group + j]
            key = keys[key_index[(delta, turn)]] + 8 * tiles * delta
            low = jnp.where(place_lane == j, key[0:1], low)
            high = jnp.where(place_lane == j, key[1:2], high)
        lows.append(low)
        highs.append(high)
    choose_slots[...] = matches(lows, highs)
    half_row = lax.shift_right_logical(row8, 1)
    heads = []
    for t in range(tiles):
        key = 8 * (tiles + t) + half_row
        heads.append(jnp.concatenate([(low == key).astype(F32) for low in lows], axis=1))
    tails = []
    for kind, found in ((full, lows), (full + 1, highs)):
        for at in (0, ROWS):
            key = jnp.where(row8 + at < tiles, 8 * (tiles + at + row8) + kind, -1)
            tails.append(jnp.concatenate([(lane == key).astype(F32) for lane in found], axis=1))
    choose_field[...] = jnp.concatenate(heads + tails, axis=0).astype(BF16)
    for f in (1, 2):
        field_bytes(f, field_recv_sem)
    start_slots = window_slots(1)
    scale_slots = window_slots(2)

    wait_slots(0, near_count, slot_recv_sem)
    back = slot_fields(choose_slots[...], received(0, near_count))
    own_found = own_back(0, near_count)
    direction_slots = start_slots + scale_slots * back
    _, solved = slot_rows(direction_slots)
    residual0 = residual0 + own_found
    direction = residual0 * scale
    product1 = block_product(direction)
    put_field(3, (product1 - diagonal * direction) * scale)
    for copy in field_copies(3):
        copy.start()
    field_bytes(1, field_send_sem)
    send_slots(1, slot_message(solved), REACH)
    field_bytes(3, field_recv_sem)
    change_slots = window_slots(3)

    wait_slots(1, near_count, slot_recv_sem)
    back = slot_fields(choose_slots[...], received(1, near_count))
    own_found = own_back(1, near_count)
    sums, solved = slot_rows(scale_slots * back - change_slots)
    send_slots(2, slot_message(solved), 1)
    field_bytes(2, field_send_sem)
    energy = energy_of(sums, solved)
    image1 = product1 - own_found
    trial = residual0 - image1
    shaped = trial * scale
    product2 = block_product(shaped)

    def lane_sum(field):
        total = field[:, :LANES]
        for i in range(1, pairs):
            total = total + field[:, i * LANES : (i + 1) * LANES]
        return jnp.sum(total, axis=0, keepdims=True) * (1.0 / grps)

    sums = jnp.zeros((ROWS, LANES), F32)
    for i, value in enumerate(
        (
            lane_sum(residual0 * direction),
            lane_sum(direction * image1),
            lane_sum(residual0 * shaped),
            lane_sum(trial * shaped),
            lane_sum(image1 * shaped),
            lane_sum(shaped * product2) - energy,
        )
    ):
        sums = jnp.where(row8 == i, value, sums)
    sums = jnp.sum(sums, axis=1, keepdims=True)
    own_sums = jnp.sum(jnp.where(row8 == lane8, sums, 0.0), axis=0, keepdims=True)
    scalar_send[...] = own_sums

    def send_scalars(index, device):
        pltpu.make_async_remote_copy(
            src_ref=scalar_send,
            dst_ref=scalar_recv.at[index],
            send_sem=scalar_sem.at[0],
            recv_sem=scalar_sem.at[1],
            device_id=device,
            device_id_type=MESH,
        ).start()

    everyone(send_scalars)

    wait_slots(2, close_count, slot_recv_sem)
    image2 = product2 - own_back(2, close_count)
    wait_bytes(scalar_recv, scalar_sem.at[1])
    totals = own_sums + jnp.sum(scalar_recv[...], axis=0)
    rz0, curve1, cross, trial_rz, mixed_sum, curve_w = [totals[:, i : i + 1] for i in range(6)]
    step1 = rz0 / curve1
    short = 1.0 - step1
    rz1 = short * short * rz0 + 2.0 * short * step1 * cross + step1 * step1 * trial_rz
    keep = short + rz1 / rz0
    curve2 = keep * keep * curve1 + 2.0 * keep * step1 * mixed_sum + step1 * step1 * curve_w
    step2 = rz1 / curve2
    near_part = step1 + step2 * keep
    far_part = step2 * step1
    solution_ref[...] = guess[...] + near_part * direction + far_part * shaped
    residual_ref[...] = residual0 - near_part * image1 - far_part * image2

    wait_bytes(scalar_recv, scalar_sem.at[0])
    for f in (0, 3):
        field_bytes(f, field_send_sem)
    wait_bytes(keys.at[first_keys], key_send_sem.at[0])
    wait_bytes(keys.at[second_keys], key_send_sem.at[1])
    for turn_no, count in enumerate((near_count, near_count, close_count)):
        wait_slots(turn_no, count, slot_send_sem)


def finish_kernel(first, second, solution_ref, residual_ref, sem):
    copies = [
        pltpu.make_async_copy(first, solution_ref, sem.at[0]),
        pltpu.make_async_copy(second, residual_ref, sem.at[1]),
    ]
    for copy in copies:
        copy.start()
    for copy in copies:
        copy.wait()


def finish(first, second):
    vmem = pl.BlockSpec(memory_space=pltpu.VMEM)
    hbm = pl.BlockSpec(memory_space=pltpu.HBM)
    shape = jax.ShapeDtypeStruct(first.shape, first.dtype)
    return pl.pallas_call(
        finish_kernel,
        out_shape=(shape, shape),
        in_specs=[vmem] * 2,
        out_specs=(hbm, hbm),
        scratch_shapes=[pltpu.SemaphoreType.DMA((2,))],
    )(*[pltpu.with_memory_space_constraint(x, pltpu.VMEM) for x in (first, second)])


def per_device(
    cells, grps, initial_guess, right_side, camera_blocks, point_inverse, jacobian_tiles, tile_pattern, cell_load
):
    params, cameras = initial_guess.shape
    slots, rows_wide, points_wide = jacobian_tiles.shape
    near = SPAN * grps
    tiles = cameras // CAM_TILE
    full = rows_wide // LANES
    field_pack = round_up(full * tiles + tiles // 2, 64)
    hbm = pl.BlockSpec(memory_space=pltpu.HBM)
    vmem = pl.BlockSpec(memory_space=pltpu.VMEM)
    dma = pltpu.SemaphoreType.DMA
    field = pltpu.VMEM((params, cameras), F32)
    first, second = pl.pallas_call(
        functools.partial(kernel, cells, grps),
        out_shape=(field, field),
        in_specs=[hbm] * 7,
        out_specs=(vmem, vmem),
        scratch_shapes=[
            pltpu.SMEM((2, slots), I32),
            pltpu.SMEM((1,), I32),
            pltpu.VMEM((params, cameras), F32),
            pltpu.VMEM((params, cameras), F32),
            pltpu.VMEM(camera_blocks.shape, F32),
            pltpu.VMEM(point_inverse.shape, F32),
            pltpu.VMEM(jacobian_tiles.shape, BF16),
            pltpu.VMEM((slots, points_wide, full * LANES), BF16),
            pltpu.VMEM((points_wide, round_up(slots // 2, 2) * LANES), BF16),
            pltpu.VMEM((4, 3, field_pack, LANES), BF16),
            pltpu.VMEM((near, 2, LANES), I32),
            pltpu.VMEM((3, PACK, LANES), BF16),
            pltpu.VMEM((3, near, PACK, LANES), BF16),
            pltpu.VMEM((1, LANES), F32),
            pltpu.VMEM((cells * grps - 1, 1, LANES), F32),
            pltpu.VMEM((ROWS * (full + 2), near * PACK), BF16),
            pltpu.VMEM((ROWS * tiles + 32, near * PACK), BF16),
            pltpu.VMEM((ROWS * (full + 2), 3 * field_pack), BF16),
            dma((6,)),
            dma((slots,)),
            dma((4,)),
            dma((4,)),
            dma((2,)),
            dma((2,)),
            dma((3,)),
            dma((3,)),
            dma((2,)),
        ],
        compiler_params=pltpu.CompilerParams(collective_id=0, has_side_effects=True),
    )(initial_guess, right_side, camera_blocks, point_inverse, jacobian_tiles, tile_pattern.T, cell_load)
    return finish(first, second)


def solution(mesh):
    placed = (
        P(None, "cell"),
        P(None, "cell"),
        P(None, None, "cell"),
        P(None, None, ("cell", "grp")),
        P(("cell", "grp"), None, None),
        P(("cell", "grp"), None),
        P("cell"),
    )
    return jax.shard_map(
        functools.partial(per_device, mesh.shape["cell"], mesh.shape["grp"]),
        mesh=mesh,
        in_specs=placed,
        out_specs=(P(None, "cell"), P(None, "cell")),
        check_vma=False,
    )
```

```python
import functools

import jax
import jax.numpy as jnp
from jax import lax
from jax.experimental import pallas as pl
from jax.experimental.pallas import tpu as pltpu
from jax.sharding import PartitionSpec as P

CAM_TILE = 64
REACH = 2
SPAN = 2 * REACH + 1
ORDER = sorted(range(-REACH, REACH + 1), key=abs)
LANES = 128
ROWS = 8
PACK = 32
NONE = -(1 << 20)
MESH = pl.DeviceIdType.MESH
F32 = jnp.float32
BF16 = jnp.bfloat16
I32 = jnp.int32


def round_up(value, step):
    return (value + step - 1) // step * step


def kernel(
    cells,
    grps,
    guess_hbm,
    right_hbm,
    blocks_hbm,
    inverse_hbm,
    jac_hbm,
    pattern_hbm,
    load_hbm,
    solution_ref,
    residual_ref,
    pattern,
    load,
    guess,
    right,
    blocks,
    inverse,
    jac,
    jac_turned,
    jac_tails,
    fields,
    keys,
    slot_send,
    slot_recv,
    scalar_send,
    scalar_recv,
    choose_slots,
    choose_field,
    choose_window,
    local_sem,
    jac_sem,
    field_send_sem,
    field_recv_sem,
    key_send_sem,
    key_recv_sem,
    slot_send_sem,
    slot_recv_sem,
    scalar_sem,
):
    params, cameras = guess.shape
    slots, rows_wide, points_wide = jac.shape
    tiles = cameras // CAM_TILE
    pairs = cameras // LANES
    coords = inverse.shape[0]
    point_tiles = inverse.shape[2] // LANES
    full = rows_wide // LANES
    slot_rows_sent = round_up(full * slots + slots // 2, 4)
    field_rows = full * tiles + tiles // 2
    field_rows_sent = round_up(field_rows, ROWS)
    field_pack = fields.shape[2]
    near_count = SPAN * grps
    close_count = 3 * grps
    devices = cells * grps
    cell = lax.axis_index("cell")
    grp = lax.axis_index("grp")

    def near(delta, turn):
        return (lax.rem(cell + delta + cells, cells), lax.rem(grp + turn + grps, grps))

    def slot_index(delta, turn):
        return ORDER.index(delta) * grps + turn % grps

    peers = sorted(
        [(d, t) for d in ORDER for t in range(grps) if (d, t) != (0, 0)],
        key=lambda peer: ((abs(peer[0]) + REACH) % (REACH + 1), -peer[1]),
    )
    first_wave = [(d, t) for d, t in peers if d == 0 or t == 0]
    second_wave = [(d, t) for d, t in peers if d != 0 and t != 0]
    key_index = {(0, 0): 0}
    for delta, turn in first_wave + second_wave:
        key_index[(delta, turn)] = len(key_index)

    turned = [lax.rem(grp + turn, grps) for turn in range(grps)]

    def everyone(act):
        for turn in range(1, grps):
            act(turn - 1, (cell, turned[turn]))

        def one_cell(delta, carry):
            other = lax.rem(cell + delta, cells)
            for turn in range(grps):
                act(delta * grps + (turn - 1), (other, turned[turn]))
            return carry

        lax.fori_loop(1, cells, one_cell, 0)

    barrier = pltpu.get_barrier_semaphore()

    def greet(index, device):
        pl.semaphore_signal(barrier, inc=1, device_id=device, device_id_type=MESH)

    if cells // 2 <= 2 * REACH:
        greeted = len(first_wave)
        for delta, turn in first_wave:
            greet(0, near(delta, turn))
    else:
        greeted = devices - 1
        everyone(greet)

    local = [
        pltpu.make_async_copy(src, dst, local_sem.at[i])
        for i, (src, dst) in enumerate(
            (
                (guess_hbm, guess),
                (pattern_hbm, pattern),
                (load_hbm, load),
                (blocks_hbm, blocks),
                (right_hbm, right),
                (inverse_hbm, inverse),
            )
        )
    ]
    jac_copies = [
        pltpu.make_async_copy(jac_hbm.at[s], jac.at[s], jac_sem.at[s]) for s in range(slots)
    ]
    for copy in local:
        copy.start()
    for copy in jac_copies:
        copy.start()

    def iota(shape, axis):
        return lax.broadcasted_iota(I32, shape, axis)

    def steps(value, width, count):
        return sum((value >= width * j).astype(I32) for j in range(1, count + 1))

    lane8 = iota((ROWS, LANES), 1)
    row8 = iota((ROWS, LANES), 0)
    low8 = lane8 < CAM_TILE
    low1 = iota((1, LANES), 1) < CAM_TILE
    even8 = lax.bitwise_and(row8, 1) == 0

    fields[:, :, field_rows_sent:, :] = jnp.zeros(
        (fields.shape[0], 3, field_pack - field_rows_sent, LANES), BF16
    )
    slot_recv[:, :, slot_rows_sent:, :] = jnp.zeros(
        (3, near_count, PACK - slot_rows_sent, LANES), BF16
    )

    pick_row = iota((field_pack, LANES), 0)
    pick_chunk = steps(pick_row, tiles, full)
    pick_tile = pick_row - pick_chunk * tiles
    pick_tail = pick_chunk == full
    source_low = 16 * pick_tile + 2 * pick_chunk
    other_tile = jnp.where(pick_tail, pick_tile + tiles // 2, pick_tile)
    flipped = other_tile + 1 - 2 * lax.bitwise_and(other_tile, 1)
    source_high = 16 * flipped + jnp.where(pick_tail, 2 * full, 2 * pick_chunk + 1)
    unused = pick_row >= field_rows
    source_low = jnp.where(unused, -1, source_low)
    source_high = jnp.where(unused, -1, source_high)
    picked_width = 16 * tiles
    lane_pick = iota((field_pack, LANES), 1)

    def one_hot(source):
        parts = [
            (source == lane_pick + LANES * j).astype(F32)
            for j in range(round_up(picked_width, LANES) // LANES)
        ]
        return jnp.concatenate(parts, axis=1)[:, :picked_width].astype(BF16)

    spread = jnp.concatenate([one_hot(source_low), one_hot(source_high)], axis=0)

    def to_rows(field):
        tall = jnp.concatenate([field, jnp.zeros((16 - params, cameras), F32)], axis=0)
        parts = []
        for i in range(pairs):
            block = tall[:, i * LANES : (i + 1) * LANES]
            parts += [block.astype(BF16), pltpu.roll(block, CAM_TILE, 1).astype(BF16)]
        both = jnp.dot(spread, jnp.concatenate(parts, axis=0), preferred_element_type=F32)
        low = lane_pick < CAM_TILE
        picked = jnp.where(low, both[:field_pack], both[field_pack:])
        return picked[:field_rows_sent].astype(BF16)

    def put_field(f, field):
        fields[f, 2, :field_rows_sent] = to_rows(field)

    def field_copies(f):
        return [
            pltpu.make_async_remote_copy(
                src_ref=fields.at[f, 2, pl.ds(0, field_rows_sent)],
                dst_ref=fields.at[f, side, pl.ds(0, field_rows_sent)],
                send_sem=field_send_sem.at[f],
                recv_sem=field_recv_sem.at[f],
                device_id=near(delta, 0),
                device_id_type=MESH,
            )
            for side, delta in ((0, 1), (1, -1))
        ]

    def wait_bytes(ref, sem):
        pltpu.make_async_copy(ref, ref, sem).wait()

    def field_bytes(f, sem):
        wait_bytes(fields.at[f, pl.ds(0, 2), pl.ds(0, field_rows_sent)], sem.at[f])

    local[0].wait()
    put_field(0, guess[...])

    local[1].wait()
    local[2].wait()
    live = [s < load[0] for s in range(slots)]
    ids = [pattern[0, s] for s in range(slots)]
    point_ids = [pattern[1, s] for s in range(slots)]
    live_rows = jnp.zeros((ROWS, LANES), I32)
    id_rows = jnp.full((ROWS, LANES), NONE, I32)
    point_rows = jnp.full((ROWS, LANES), -1, I32)
    first_rows = jnp.zeros((ROWS, LANES), F32)
    for s in range(slots):
        here = row8 == s
        id_rows = jnp.where(here, jnp.where(live[s], 8 * ids[s], NONE), id_rows)
        point_rows = jnp.where(here, point_ids[s], point_rows)
        live_rows = jnp.where(here, jnp.where(live[s], 1, 0), live_rows)
        first = live[s]
        for u in range(s):
            same = jnp.logical_and(live[u], point_ids[u] == point_ids[s])
            first = jnp.logical_and(first, jnp.logical_not(same))
        first_rows = jnp.where(here, jnp.where(first, 1.0, 0.0), first_rows)
    live8 = live_rows > 0
    shared = [
        jnp.logical_and(point_rows == point_ids[s], jnp.where(live[s], 1, 0) > 0)
        for s in range(slots)
    ]

    key_lane = lax.bitwise_and(iota((2, LANES), 1), PACK - 1)
    key_chunk = steps(key_lane, slots, full)
    key_slot = key_lane - slots * key_chunk
    key_row = iota((2, LANES), 0)
    key_tail = jnp.logical_and(key_chunk == full, key_slot < slots // 2)
    own_key = jnp.full((2, LANES), NONE, I32)
    for s in range(slots):
        code = jnp.where(live[s], 8 * ids[s], NONE)
        head = jnp.logical_and(jnp.logical_and(key_chunk < full, key_slot == s), key_row == 0)
        tail_row, tail_slot = divmod(s, slots // 2)
        tail = jnp.logical_and(
            jnp.logical_and(key_tail, key_slot == tail_slot), key_row == tail_row
        )
        own_key = jnp.where(head, code + key_chunk, own_key)
        own_key = jnp.where(tail, code + full + tail_row, own_key)
    keys[0] = own_key

    row_keys = [id_rows + b for b in range(full + 2)]

    window_lane = iota((1, LANES), 1)
    window_parts = [[], []]
    window_width = 3 * field_pack
    for group in range(round_up(window_width, LANES) // LANES):
        position = window_lane + LANES * group
        place = steps(position, field_pack, 2)
        side = jnp.where(place == 0, 0, jnp.where(place == 1, 2, 1))
        row = position - place * field_pack
        chunk = steps(row, tiles, full)
        tile = side * tiles + row - chunk * tiles
        off = row >= field_rows
        tail = jnp.logical_and(chunk == full, jnp.logical_not(off))
        window_parts[0].append(jnp.where(off, -1, 8 * tile + chunk))
        window_parts[1].append(jnp.where(tail, 8 * (tile + tiles // 2) + full + 1, -1))
    window_low = window_parts[0]
    window_high = window_parts[1]

    def matches(low_keys, high_keys):
        parts = []
        for b in range(full + 2):
            found = low_keys if b <= full else high_keys
            parts.append(
                jnp.concatenate([(key == row_keys[b]).astype(F32) for key in found], axis=1)
            )
        return jnp.concatenate(parts, axis=0).astype(BF16)

    choose_window[...] = matches(window_low, window_high)[:, :window_width]

    def slot_fields(chosen, rows):
        found = jnp.dot(chosen, rows, preferred_element_type=F32)
        parts = [found[b * ROWS : (b + 1) * ROWS] for b in range(full + 2)]
        tail = parts[full] + pltpu.roll(parts[full + 1], CAM_TILE, 1)
        return jnp.concatenate(parts[:full] + [tail], axis=1)[:, :rows_wide]

    def window_slots(f):
        return slot_fields(choose_window[...], fields[f].reshape(window_width, LANES))

    def block_product(field):
        total = blocks[0] * field[0:1, :]
        for k in range(1, params):
            total = total + blocks[k] * field[k : k + 1, :]
        return total

    local[3].wait()
    row_wide = iota((params, cameras), 0)
    diagonal = blocks[0]
    for k in range(1, params):
        diagonal = jnp.where(row_wide == k, blocks[k], diagonal)
    scale = 1.0 / diagonal
    local[4].wait()
    residual0 = right[...] - block_product(guess[...])
    put_field(1, residual0 * scale)
    put_field(2, scale)
    local[5].wait()
    inverse_rows = []
    for j in range(coords):
        for i in range(coords):
            picked = jnp.zeros((ROWS, LANES), F32)
            for q in range(point_tiles):
                picked = jnp.where(
                    point_rows == q, inverse[j, i : i + 1, q * LANES : (q + 1) * LANES], picked
                )
            inverse_rows.append(picked)

    for copy in jac_copies:
        copy.wait()
    pl.semaphore_wait(barrier, greeted)

    for copy in field_copies(0):
        copy.start()

    def send_keys(wave, sem):
        for delta, turn in wave:
            pltpu.make_async_remote_copy(
                src_ref=keys.at[0],
                dst_ref=keys.at[key_index[(-delta, -turn % grps)]],
                send_sem=key_send_sem.at[sem],
                recv_sem=key_recv_sem.at[sem],
                device_id=near(delta, turn),
                device_id_type=MESH,
            ).start()

    first_keys = pl.ds(1, len(first_wave))
    second_keys = pl.ds(1 + len(first_wave), len(second_wave))
    send_keys(first_wave, 0)
    for f in (1, 2):
        for copy in field_copies(f):
            copy.start()
    wide = full * LANES
    for s in range(slots):
        jac_turned[s] = jac[s, :wide].T
    spare = jac_tails.shape[1] - slots // 2 * LANES
    if spare:
        jac_tails[:, slots // 2 * LANES :] = jnp.zeros((points_wide, spare), BF16)
    for i in range(slots // 2):
        both = jnp.concatenate([jac[i, wide:], jac[i + slots // 2, wide:]], axis=0)
        jac_tails[:, i * LANES : (i + 1) * LANES] = both.T

    def slot_rows(values):
        values = jnp.where(live_wide, values, 0.0)
        half = slots // 2
        wide = full * LANES
        split = points_wide // (2 * LANES) * (2 * LANES)
        rows = [jnp.where(shared_wide[s], values[s : s + 1, :], 0.0) for s in range(slots)]
        rest = jnp.concatenate([row[:, wide:].astype(BF16) for row in rows], axis=1)
        tail = jnp.dot(
            rest,
            jnp.concatenate([jac[s, wide:] for s in range(slots)], axis=0),
            preferred_element_type=F32,
        )
        left = jnp.zeros((ROWS, split), F32)
        right = jnp.zeros((ROWS, points_wide - split), F32)
        for i in range(half):
            u = i + half
            both = jnp.concatenate([rows[i][:, :wide], rows[u][:, :wide]], axis=0).astype(BF16)
            found = jnp.dot(
                both,
                jnp.concatenate([jac[i, :wide], jac[u, :wide]], axis=1),
                preferred_element_type=F32,
            )
            total = found[:ROWS, :points_wide] + found[ROWS:, points_wide:]
            left = left + total[:, :split]
            right = right + total[:, split:]
        sums = jnp.concatenate([left, right], axis=1) + tail
        solved = []
        for j in range(coords):
            total = inverse_rows[j * coords] * sums[:, :LANES]
            for i in range(1, coords):
                total = total + inverse_rows[j * coords + i] * sums[:, i * LANES : (i + 1) * LANES]
            solved.append(total)
        solved = jnp.concatenate(solved, axis=1).astype(BF16).astype(F32)
        return sums, solved

    def slot_message(solved):
        parts = [jnp.zeros((ROWS, LANES), F32) for _ in range(PACK // ROWS)]
        for s in range(slots):
            row = jnp.broadcast_to(solved[s : s + 1, :], (ROWS, points_wide)).astype(BF16)
            product = jnp.dot(row, jac_turned[s], preferred_element_type=F32)
            product = jnp.where(live[s], product, 0.0)
            for b in range(full):
                at, inside = divmod(b * slots + s, ROWS)
                parts[at] = jnp.where(
                    row8 == inside, product[:, b * LANES : (b + 1) * LANES], parts[at]
                )
        shorts = jnp.dot(solved.astype(BF16), jac_tails[...], preferred_element_type=F32)
        for i in range(slots // 2):
            at, inside = divmod(full * slots + i, ROWS)
            product = jnp.where(live8, shorts[:, i * LANES : (i + 1) * LANES], 0.0)
            other = i + slots // 2
            both = jnp.where(low1, product[i : i + 1], product[other : other + 1])
            parts[at] = jnp.where(row8 == inside, both, parts[at])
        return jnp.concatenate(parts, axis=0).astype(BF16)

    def energy_of(sums, solved):
        energy = sums * solved
        lanes = energy[:, :LANES]
        for i in range(1, coords):
            lanes = lanes + energy[:, i * LANES : (i + 1) * LANES]
        return jnp.sum(lanes * first_rows, axis=0, keepdims=True)

    live_wide = jnp.concatenate([live8] * (full + 1), axis=1)[:, :rows_wide]
    shared_wide = [
        jnp.concatenate([shared[s]] * (full + 1), axis=1)[:, :rows_wide] for s in range(slots)
    ]

    def send_slots(turn_no, message, reach):
        slot_send[turn_no] = message
        slot_recv[turn_no, 0] = message
        for delta, turn in peers:
            if abs(delta) <= reach:
                pltpu.make_async_remote_copy(
                    src_ref=slot_send.at[turn_no, pl.ds(0, slot_rows_sent)],
                    dst_ref=slot_recv.at[
                        turn_no, slot_index(-delta, -turn), pl.ds(0, slot_rows_sent)
                    ],
                    send_sem=slot_send_sem.at[turn_no],
                    recv_sem=slot_recv_sem.at[turn_no],
                    device_id=near(delta, turn),
                    device_id_type=MESH,
                ).start()

    def wait_slots(turn_no, count, sem):
        wait_bytes(
            slot_recv.at[turn_no, pl.ds(1, count - 1), pl.ds(0, slot_rows_sent)], sem.at[turn_no]
        )

    def received(turn_no, count):
        return slot_recv[turn_no, :count].reshape(count * PACK, LANES)

    def own_back(turn_no, count):
        width = count * PACK
        found = jnp.dot(
            choose_field[:, :width], received(turn_no, count), preferred_element_type=F32
        )
        tail_low = found[ROWS * tiles : ROWS * tiles + 16]
        tail_high = found[ROWS * tiles + 16 : ROWS * tiles + 32]
        lasts_low = tail_low + pltpu.roll(tail_high, CAM_TILE, 1)
        lasts_high = pltpu.roll(tail_low, CAM_TILE, 1) + tail_high
        parts = []
        for i in range(pairs):
            first = found[2 * ROWS * i : 2 * ROWS * i + ROWS]
            second = found[2 * ROWS * i + ROWS : 2 * ROWS * (i + 1)]
            top = jnp.where(
                low8,
                jnp.where(even8, first, pltpu.roll(first, CAM_TILE, 1)),
                jnp.where(even8, pltpu.roll(second, CAM_TILE, 1), second),
            )
            last = jnp.where(
                low1, lasts_low[2 * i : 2 * i + 1], lasts_high[2 * i + 1 : 2 * i + 2]
            )
            parts.append(jnp.concatenate([top, last], axis=0))
        return jnp.concatenate(parts, axis=1)

    field_bytes(0, field_recv_sem)
    wait_bytes(keys.at[first_keys], key_recv_sem.at[0])
    _, solved = slot_rows(window_slots(0))
    send_keys(second_wave, 1)
    send_slots(0, slot_message(solved), REACH)

    wait_bytes(keys.at[second_keys], key_recv_sem.at[1])
    lows, highs = [], []
    place_lane = lax.shift_right_logical(window_lane, 5)
    per_group = LANES // PACK
    order = [(delta, turn) for delta in ORDER for turn in range(grps)]
    for group in range(near_count // per_group):
        low = jnp.full((1, LANES), NONE, I32)
        high = jnp.full((1, LANES), NONE, I32)
        for j in range(per_group):
            delta, turn = order[group * per_group + j]
            key = keys[key_index[(delta, turn)]] + 8 * tiles * delta
            low = jnp.where(place_lane == j, key[0:1], low)
            high = jnp.where(place_lane == j, key[1:2], high)
        lows.append(low)
        highs.append(high)
    choose_slots[...] = matches(lows, highs)
    half_row = lax.shift_right_logical(row8, 1)
    heads = []
    for t in range(tiles):
        key = 8 * (tiles + t) + half_row
        heads.append(jnp.concatenate([(low == key).astype(F32) for low in lows], axis=1))
    tails = []
    for kind, found in ((full, lows), (full + 1, highs)):
        for at in (0, ROWS):
            key = jnp.where(row8 + at < tiles, 8 * (tiles + at + row8) + kind, -1)
            tails.append(jnp.concatenate([(lane == key).astype(F32) for lane in found], axis=1))
    choose_field[...] = jnp.concatenate(heads + tails, axis=0).astype(BF16)
    for f in (1, 2):
        field_bytes(f, field_recv_sem)
    start_slots = window_slots(1)
    scale_slots = window_slots(2)

    wait_slots(0, near_count, slot_recv_sem)
    back = slot_fields(choose_slots[...], received(0, near_count))
    own_found = own_back(0, near_count)
    direction_slots = start_slots + scale_slots * back
    _, solved = slot_rows(direction_slots)
    residual0 = residual0 + own_found
    direction = residual0 * scale
    product1 = block_product(direction)
    put_field(3, (product1 - diagonal * direction) * scale)
    for copy in field_copies(3):
        copy.start()
    field_bytes(1, field_send_sem)
    send_slots(1, slot_message(solved), REACH)
    field_bytes(3, field_recv_sem)
    change_slots = window_slots(3)

    wait_slots(1, near_count, slot_recv_sem)
    back = slot_fields(choose_slots[...], received(1, near_count))
    own_found = own_back(1, near_count)
    sums, solved = slot_rows(scale_slots * back - change_slots)
    send_slots(2, slot_message(solved), 1)
    field_bytes(2, field_send_sem)
    energy = energy_of(sums, solved)
    image1 = product1 - own_found
    trial = residual0 - image1
    shaped = trial * scale
    product2 = block_product(shaped)

    def lane_sum(field):
        total = field[:, :LANES]
        for i in range(1, pairs):
            total = total + field[:, i * LANES : (i + 1) * LANES]
        return jnp.sum(total, axis=0, keepdims=True) * (1.0 / grps)

    sums = jnp.zeros((ROWS, LANES), F32)
    for i, value in enumerate(
        (
            lane_sum(residual0 * direction),
            lane_sum(direction * image1),
            lane_sum(residual0 * shaped),
            lane_sum(trial * shaped),
            lane_sum(image1 * shaped),
            lane_sum(shaped * product2) - energy,
        )
    ):
        sums = jnp.where(row8 == i, value, sums)
    sums = jnp.sum(sums, axis=1, keepdims=True)
    own_sums = jnp.sum(jnp.where(row8 == lane8, sums, 0.0), axis=0, keepdims=True)
    scalar_send[...] = own_sums

    def send_scalars(index, device):
        pltpu.make_async_remote_copy(
            src_ref=scalar_send,
            dst_ref=scalar_recv.at[index],
            send_sem=scalar_sem.at[0],
            recv_sem=scalar_sem.at[1],
            device_id=device,
            device_id_type=MESH,
        ).start()

    everyone(send_scalars)

    wait_slots(2, close_count, slot_recv_sem)
    image2 = product2 - own_back(2, close_count)
    wait_bytes(scalar_recv, scalar_sem.at[1])
    totals = own_sums + jnp.sum(scalar_recv[...], axis=0)
    rz0, curve1, cross, trial_rz, mixed_sum, curve_w = [totals[:, i : i + 1] for i in range(6)]
    step1 = rz0 / curve1
    short = 1.0 - step1
    rz1 = short * short * rz0 + 2.0 * short * step1 * cross + step1 * step1 * trial_rz
    keep = short + rz1 / rz0
    curve2 = keep * keep * curve1 + 2.0 * keep * step1 * mixed_sum + step1 * step1 * curve_w
    step2 = rz1 / curve2
    near_part = step1 + step2 * keep
    far_part = step2 * step1
    solution_ref[...] = guess[...] + near_part * direction + far_part * shaped
    residual_ref[...] = residual0 - near_part * image1 - far_part * image2

    wait_bytes(scalar_recv, scalar_sem.at[0])
    for f in (0, 3):
        field_bytes(f, field_send_sem)
    wait_bytes(keys.at[first_keys], key_send_sem.at[0])
    wait_bytes(keys.at[second_keys], key_send_sem.at[1])
    for turn_no, count in enumerate((near_count, near_count, close_count)):
        wait_slots(turn_no, count, slot_send_sem)


def finish_kernel(first, second, solution_ref, residual_ref, sem):
    copies = [
        pltpu.make_async_copy(first, solution_ref, sem.at[0]),
        pltpu.make_async_copy(second, residual_ref, sem.at[1]),
    ]
    for copy in copies:
        copy.start()
    for copy in copies:
        copy.wait()


def finish(first, second):
    vmem = pl.BlockSpec(memory_space=pltpu.VMEM)
    hbm = pl.BlockSpec(memory_space=pltpu.HBM)
    shape = jax.ShapeDtypeStruct(first.shape, first.dtype)
    return pl.pallas_call(
        finish_kernel,
        out_shape=(shape, shape),
        in_specs=[vmem] * 2,
        out_specs=(hbm, hbm),
        scratch_shapes=[pltpu.SemaphoreType.DMA((2,))],
    )(*[pltpu.with_memory_space_constraint(x, pltpu.VMEM) for x in (first, second)])


def per_device(
    cells, grps, initial_guess, right_side, camera_blocks, point_inverse, jacobian_tiles, tile_pattern, cell_load
):
    params, cameras = initial_guess.shape
    slots, rows_wide, points_wide = jacobian_tiles.shape
    near = SPAN * grps
    tiles = cameras // CAM_TILE
    full = rows_wide // LANES
    field_pack = round_up(full * tiles + tiles // 2, 64)
    hbm = pl.BlockSpec(memory_space=pltpu.HBM)
    vmem = pl.BlockSpec(memory_space=pltpu.VMEM)
    dma = pltpu.SemaphoreType.DMA
    field = pltpu.VMEM((params, cameras), F32)
    first, second = pl.pallas_call(
        functools.partial(kernel, cells, grps),
        out_shape=(field, field),
        in_specs=[hbm] * 7,
        out_specs=(vmem, vmem),
        scratch_shapes=[
            pltpu.SMEM((2, slots), I32),
            pltpu.SMEM((1,), I32),
            pltpu.VMEM((params, cameras), F32),
            pltpu.VMEM((params, cameras), F32),
            pltpu.VMEM(camera_blocks.shape, F32),
            pltpu.VMEM(point_inverse.shape, F32),
            pltpu.VMEM(jacobian_tiles.shape, BF16),
            pltpu.VMEM((slots, points_wide, full * LANES), BF16),
            pltpu.VMEM((points_wide, round_up(slots // 2, 2) * LANES), BF16),
            pltpu.VMEM((4, 3, field_pack, LANES), BF16),
            pltpu.VMEM((near, 2, LANES), I32),
            pltpu.VMEM((3, PACK, LANES), BF16),
            pltpu.VMEM((3, near, PACK, LANES), BF16),
            pltpu.VMEM((1, LANES), F32),
            pltpu.VMEM((cells * grps - 1, 1, LANES), F32),
            pltpu.VMEM((ROWS * (full + 2), near * PACK), BF16),
            pltpu.VMEM((ROWS * tiles + 32, near * PACK), BF16),
            pltpu.VMEM((ROWS * (full + 2), 3 * field_pack), BF16),
            dma((6,)),
            dma((slots,)),
            dma((4,)),
            dma((4,)),
            dma((2,)),
            dma((2,)),
            dma((3,)),
            dma((3,)),
            dma((2,)),
        ],
        compiler_params=pltpu.CompilerParams(collective_id=0, has_side_effects=True),
    )(initial_guess, right_side, camera_blocks, point_inverse, jacobian_tiles, tile_pattern.T, cell_load)
    return finish(first, second)


def solution(mesh):
    placed = (
        P(None, "cell"),
        P(None, "cell"),
        P(None, None, "cell"),
        P(None, None, ("cell", "grp")),
        P(("cell", "grp"), None, None),
        P(("cell", "grp"), None),
        P("cell"),
    )
    return jax.shard_map(
        functools.partial(per_device, mesh.shape["cell"], mesh.shape["grp"]),
        mesh=mesh,
        in_specs=placed,
        out_specs=(P(None, "cell"), P(None, "cell")),
        check_vma=False,
    )
```
